32 devices in a mesh: ctx: 2 (over x), hs: 16 (over z, y, core).
Axes of the slice: x: 2, y: 2, z: 4, core: 2. Of those that a mesh axis runs over, the one named last changes fastest.
Arguments:
- key_rows: bfloat16 [16, 1024, 512], P('hs', 'ctx'), may hold values from -6 to 6
- value_rows: bfloat16 [16, 1024, 512], P('hs', 'ctx'), may hold values from -6 to 6
- query_rows: bfloat16 [16, 1024, 512], P('hs', 'ctx'), may hold values from -6 to 6
- step_rates: float32 [16, 1024], P('hs', 'ctx'), may hold values from 0.0003 to 0.003
- fast_gate: bfloat16 [16, 512, 512], P('hs', 'ctx'), may hold values from -0.25 to 0.25
- fast_up: bfloat16 [16, 512, 512], P('hs', 'ctx'), may hold values from -0.25 to 0.25
- fast_down: bfloat16 [16, 512, 512], P('hs', 'ctx'), may hold values from -0.25 to 0.25
- out_gain: float32 [2048], replicated, may hold values from 0.1 to 1.9
- gate_input: bfloat16 [1024, 4, 2048], P(('ctx', 'hs')), may hold values from -6 to 6
- out_weight: bfloat16 [2048, 1024], P('hs'), may hold values from -0.125 to 0.125
Outputs:
- layer_out: bfloat16 [1024, 4, 1024], P(('ctx', 'hs'))
The draws below stay inside these ranges and needn't reach their ends.
All inputs are finite; a program needn't handle non-finite values.
Results may differ from the reference program's by a relative error of at most 0.01.
Values may be sent and summed in bfloat16 or wider, within the bound.
A program may use at most 64 MiB of HBM per device.

```python
import math
import jax
import jax.numpy as jnp
from jax import lax

D = 2048
HEADS = 4
DH = 512
FH = 512
DOUT = 1024
GROUP = 1024
SEQS = 4
PAIRS = 16


def level_of(own_key, shape, shards, low, largest):
    gain, own = 1.0, jax.random.fold_in(own_key, 6)
    for position, blocks in shards:
        draws = jnp.exp(jax.random.uniform(jax.random.fold_in(own, position), (blocks,), jnp.float32, low / len(shards), largest / len(shards)))
        gain = gain * jnp.repeat(draws, shape[position] // blocks).reshape([-1 if axis == position else 1 for axis in range(len(shape))])
    return gain


def centred(key, extent, scale, limit, pieces=(), dtype=jnp.bfloat16):
    drawn = jax.random.normal(key, extent, jnp.float32) * scale
    if len(pieces) > 0:
        drawn = level_of(key, extent, pieces, -0.22, 0.18) * drawn
    return jnp.clip(drawn, min=-limit, max=limit).astype(dtype)


def setup_inputs(seed: int = 0) -> dict:
    arg_keys = jax.random.split(jax.random.key(seed), 11)
    key_rows = centred(arg_keys[0], (PAIRS, GROUP, DH), 1.0, 6.0, ((0, 16), (1, 2)))
    value_rows = centred(arg_keys[1], (PAIRS, GROUP, DH), 1.0, 6.0, ((0, 16), (1, 2)))
    query_rows = centred(arg_keys[2], (PAIRS, GROUP, DH), 1.0, 6.0, ((0, 16), (1, 2)))
    step_rates = jnp.clip(jnp.exp(math.log(0.003) - 2.3025851 * jax.random.uniform(arg_keys[3], (PAIRS, GROUP), jnp.float32) ** level_of(arg_keys[3], (PAIRS, GROUP), ((0, 16), (1, 2)), -0.2, 0.2)), 0.0003, 0.003)
    fast_gate = centred(arg_keys[4], (PAIRS, FH, DH), DH ** -0.5, 0.25, ((0, 16), (1, 2)))
    fast_up = centred(arg_keys[5], (PAIRS, FH, DH), DH ** -0.5, 0.25, ((0, 16), (1, 2)))
    fast_down = centred(arg_keys[6], (PAIRS, DH, FH), FH ** -0.5, 0.25, ((0, 16), (1, 2)))
    out_gain = jnp.clip(1.0 + 0.18 * jax.random.normal(arg_keys[7], (D,), jnp.float32), 0.1, 1.9)
    gate_input = centred(arg_keys[8], (GROUP, SEQS, D), 1.0, 6.0, ((0, 32),))
    out_weight = centred(arg_keys[9], (D, DOUT), D ** -0.5, 0.125, ((0, 16),))
    return dict(key_rows=key_rows, value_rows=value_rows, query_rows=query_rows, step_rates=step_rates, fast_gate=fast_gate, fast_up=fast_up, fast_down=fast_down, out_gain=out_gain, gate_input=gate_input, out_weight=out_weight)


epsilon = 1e-06

def rescale_rows(weight, update):
    base = weight.astype(jnp.float32)
    moved = base + update
    factor = jnp.sqrt(lax.optimization_barrier(jnp.mean(base * base, -1, keepdims=True)) + epsilon) / jnp.sqrt(lax.optimization_barrier(jnp.mean(moved * moved, -1, keepdims=True)) + epsilon)
    return (moved * factor).astype(jnp.bfloat16)

def inner_rows(left, right):
    return lax.dot_general(left, right, (((0,), (0,)), ((), ())), preferred_element_type=jnp.float32)

def one_pair(packed):
    key_row, value_row, query_row, rate_row, gate_fast, up_fast, down_fast = packed
    pre_gate = jnp.dot(key_row, gate_fast.T, preferred_element_type=jnp.float32)
    pre_up = jnp.dot(key_row, up_fast.T, preferred_element_type=jnp.float32)
    sig_gate = jax.nn.sigmoid(pre_gate)
    act_gate = pre_gate * sig_gate
    hidden = (act_gate * pre_up).astype(jnp.bfloat16)
    scaled = (rate_row[:, None] * value_row.astype(jnp.float32)).astype(jnp.bfloat16)
    grad_down = inner_rows(scaled, hidden)
    back_hidden = jnp.dot(scaled, down_fast, preferred_element_type=jnp.float32)
    back_gate = (back_hidden * pre_up * sig_gate * (1.0 + pre_gate * (1.0 - sig_gate))).astype(jnp.bfloat16)
    back_up = (back_hidden * act_gate).astype(jnp.bfloat16)
    grad_gate = inner_rows(back_gate, key_row)
    grad_up = inner_rows(back_up, key_row)
    new_gate = rescale_rows(gate_fast, grad_gate)
    new_up = rescale_rows(up_fast, grad_up)
    new_down = rescale_rows(down_fast, grad_down)
    query_gate = jnp.dot(query_row, new_gate.T, preferred_element_type=jnp.float32)
    query_up = jnp.dot(query_row, new_up.T, preferred_element_type=jnp.float32)
    query_hidden = (jax.nn.silu(query_gate) * query_up).astype(jnp.bfloat16)
    return jnp.dot(query_hidden, new_down.T, preferred_element_type=jnp.float32).astype(jnp.bfloat16)

def reference(key_rows, value_rows, query_rows, step_rates, fast_gate, fast_up, fast_down, out_gain, gate_input, out_weight):
    head_out = lax.map(one_pair, (key_rows, value_rows, query_rows, step_rates, fast_gate, fast_up, fast_down))
    mixed = head_out.reshape(SEQS, HEADS, GROUP, DH).transpose(2, 0, 1, 3).astype(jnp.float32)
    square = lax.optimization_barrier(jnp.mean(mixed * mixed, -1, keepdims=True))
    scaled_heads = mixed * lax.rsqrt(square + epsilon) * out_gain.reshape(HEADS, DH)
    normed = (scaled_heads.reshape(GROUP, SEQS, D) * jax.nn.silu(gate_input.astype(jnp.float32))).astype(jnp.bfloat16)
    result = jnp.dot(normed.reshape(GROUP * SEQS, D), out_weight, preferred_element_type=jnp.float32)
    return result.astype(jnp.bfloat16).reshape(GROUP, SEQS, DOUT)
```

```python
import functools

import jax
import jax.numpy as jnp
from jax import lax
from jax.experimental import pallas as pl
from jax.experimental.pallas import tpu as pltpu
from jax.sharding import PartitionSpec as P

epsilon = 1e-06


def rescale_rows(weight, update):
    base = weight.astype(jnp.float32)
    moved = base + update
    factor = jnp.sqrt(jnp.mean(base * base, -1, keepdims=True) + epsilon) / jnp.sqrt(
        jnp.mean(moved * moved, -1, keepdims=True) + epsilon
    )
    return (moved * factor).astype(jnp.bfloat16)


def inner_rows(left, right):
    return lax.dot_general(
        left, right, (((0,), (0,)), ((), ())), preferred_element_type=jnp.float32
    )


def body(
    key_rows,
    value_rows,
    query_rows,
    step_rates,
    fast_gate,
    fast_up,
    fast_down,
    out_gain,
    gate_input,
    out_weight,
):
    key_row = key_rows[0]
    value_row = value_rows[0]
    query_row = query_rows[0]
    rate_row = step_rates[0]
    whole_gate, whole_up, whole_down = (
        lax.all_gather(fast_gate, "ctx", axis=1, tiled=True),
        lax.all_gather(fast_up, "ctx", axis=1, tiled=True),
        lax.all_gather(fast_down, "ctx", axis=1, tiled=True),
    )
    gate_fast = whole_gate[0]
    up_fast = whole_up[0]
    down_fast = whole_down[0]
    pre_gate = jnp.dot(key_row, gate_fast.T, preferred_element_type=jnp.float32)
    pre_up = jnp.dot(key_row, up_fast.T, preferred_element_type=jnp.float32)
    sig_gate = jax.nn.sigmoid(pre_gate)
    act_gate = pre_gate * sig_gate
    hidden = (act_gate * pre_up).astype(jnp.bfloat16)
    scaled = (rate_row[:, None] * value_row.astype(jnp.float32)).astype(jnp.bfloat16)
    grad_down = inner_rows(scaled, hidden)
    back_hidden = jnp.dot(scaled, down_fast, preferred_element_type=jnp.float32)
    back_gate = (back_hidden * pre_up * sig_gate * (1.0 + pre_gate * (1.0 - sig_gate))).astype(
        jnp.bfloat16
    )
    back_up = (back_hidden * act_gate).astype(jnp.bfloat16)
    grad_gate = inner_rows(back_gate, key_row)
    grad_up = inner_rows(back_up, key_row)
    grad_gate, grad_up, grad_down = (
        lax.psum_scatter(grad_gate, "ctx", scatter_dimension=0, tiled=True),
        lax.psum_scatter(grad_up, "ctx", scatter_dimension=0, tiled=True),
        lax.psum_scatter(grad_down, "ctx", scatter_dimension=0, tiled=True),
    )
    part_gate = rescale_rows(fast_gate[0], grad_gate)
    part_up = rescale_rows(fast_up[0], grad_up)
    part_down = rescale_rows(fast_down[0], grad_down)
    new_gate, new_up, new_down = (
        lax.all_gather(part_gate, "ctx", axis=0, tiled=True),
        lax.all_gather(part_up, "ctx", axis=0, tiled=True),
        lax.all_gather(part_down, "ctx", axis=0, tiled=True),
    )
    query_gate = jnp.dot(query_row, new_gate.T, preferred_element_type=jnp.float32)
    query_up = jnp.dot(query_row, new_up.T, preferred_element_type=jnp.float32)
    query_hidden = (jax.nn.silu(query_gate) * query_up).astype(jnp.bfloat16)
    head_out = jnp.dot(query_hidden, new_down.T, preferred_element_type=jnp.float32).astype(
        jnp.bfloat16
    )
    width_hs = lax.axis_size("hs")
    head_size = head_out.shape[1]
    token_count = head_out.shape[0] // width_hs
    blocks = head_out.reshape(width_hs, token_count, head_size)
    moved = lax.all_to_all(blocks, "hs", split_axis=0, concat_axis=2, tiled=True)
    seq_count = gate_input.shape[1]
    model_width = gate_input.shape[2]
    head_count = model_width // head_size
    mixed = moved.reshape(token_count, seq_count, head_count, head_size).astype(jnp.float32)
    square = jnp.mean(mixed * mixed, -1, keepdims=True)
    scaled_heads = mixed * lax.rsqrt(square + epsilon) * out_gain.reshape(head_count, head_size)
    normed = (
        scaled_heads.reshape(token_count, seq_count, model_width)
        * jax.nn.silu(gate_input.astype(jnp.float32))
    ).astype(jnp.bfloat16)
    flat_rows = normed.reshape(token_count * seq_count, model_width)
    out_cols = out_weight.shape[1]
    full_weight = lax.all_gather(out_weight, "hs", axis=0, tiled=True)
    result = jnp.dot(flat_rows, full_weight, preferred_element_type=jnp.float32)
    return result.astype(jnp.bfloat16).reshape(token_count, seq_count, out_cols)


MESH = pl.DeviceIdType.MESH


def inner_cols(left, right):
    return lax.dot_general(
        left, right, (((1,), (1,)), ((), ())), preferred_element_type=jnp.float32
    )


def layer_kernel(
    layers,
    pieces,
    gate_hbm,
    up_hbm,
    down_hbm,
    key_hbm,
    value_hbm,
    query_hbm,
    side_hbm,
    weight_hbm,
    rate_ref,
    gain_ref,
    out_ref,
    fast,
    fresh,
    keys,
    values,
    rates,
    queries,
    side,
    opened,
    full,
    grads,
    heads,
    mixed,
    normed,
    laid,
    local_sem,
    ctx_send,
    ctx_recv,
    full_send,
    full_recv,
    head_send,
    head_recv,
    fresh_send,
    fresh_recv,
    ready,
):
    ctx = lax.axis_index("ctx")
    me = lax.axis_index("hs")
    other = 1 - ctx
    count = 4 * layers
    depth, inner = me // 4, me % 4
    row, core = inner // 2, inner % 2
    row_peer = depth * 4 + (1 - row) * 2 + core
    core_peer = depth * 4 + row * 2 + (1 - core)
    pair = depth * 4 + row * 2 + ctx
    owner = core == ctx
    helper = core != ctx

    def remote(source, target, send, recv, device):
        return pltpu.make_async_remote_copy(
            src_ref=source,
            dst_ref=target,
            send_sem=send,
            recv_sem=recv,
            device_id=device,
            device_id_type=MESH,
        )

    part = gate_hbm.shape[1]
    tokens = key_hbm.shape[1]
    piece = tokens // pieces
    shard = weight_hbm.shape[0]

    def rows(start, size):
        return pl.ds(pl.multiple_of(start, size), size)

    def guarded(condition, action):
        if condition is None:
            action()
        else:
            pl.when(condition)(action)

    weights = (gate_hbm, up_hbm, down_hbm)
    local = []
    for i, source in enumerate(weights):
        local.append(
            pltpu.make_async_copy(source.at[0], fast.at[i, rows(ctx * part, part)], local_sem.at[i])
        )
    local.append(
        pltpu.make_async_copy(key_hbm.at[0], keys.at[rows(ctx * tokens, tokens)], local_sem.at[3])
    )
    local.append(
        pltpu.make_async_copy(value_hbm.at[0], values.at[rows(ctx * tokens, tokens)], local_sem.at[4])
    )
    local.append(pltpu.make_async_copy(weight_hbm, full.at[rows(me * shard, shard)], local_sem.at[5]))
    local.append(pltpu.make_async_copy(query_hbm.at[0], queries, local_sem.at[6]))
    local.append(pltpu.make_async_copy(side_hbm, side, local_sem.at[7]))
    owned = [0, 1, 2, 3, 4, 6]
    for i in (5, 7):
        local[i].start()

    @pl.when(owner)
    def _():
        for i in owned:
            local[i].start()

    last = layers - 1
    links = [
        (None, {"ctx": other}),
        (None, {"hs": row_peer}),
        (None, {"hs": core_peer}),
        (depth < last, {"hs": me + 4}),
        (depth > 0, {"hs": me - 4}),
    ]
    link_count = 3 + jnp.where(depth < last, 1, 0) + jnp.where(depth > 0, 1, 0)

    def greet(semaphore):
        for condition, device in links:
            guarded(
                condition,
                functools.partial(
                    pl.semaphore_signal, semaphore, inc=1, device_id=device, device_id_type=MESH
                ),
            )

    barrier = pltpu.get_barrier_semaphore()
    greet(barrier)
    pl.semaphore_signal(
        barrier, inc=1, device_id={"ctx": other, "hs": core_peer}, device_id_type=MESH
    )
    pl.semaphore_wait(barrier, link_count + 1)

    swaps = []
    for i, source in enumerate(weights):
        swaps.append((source.at[0], lambda who, i=i: fast.at[i, rows(who * part, part)]))
    for j in range(pieces):
        for source, target in ((key_hbm.at[0], keys), (value_hbm.at[0], values)):
            swaps.append(
                (
                    source.at[pl.ds(j * piece, piece)],
                    lambda who, target=target, j=j: target.at[
                        rows(who * tokens + j * piece, piece)
                    ],
                )
            )
    swaps.append((rate_ref, lambda who: rates))
    outgoing = [
        remote(source, target(ctx), ctx_send.at[i], ctx_recv.at[i], {"ctx": other})
        for i, (source, target) in enumerate(swaps)
    ]
    incoming = [
        remote(source, target(other), ctx_send.at[i], ctx_recv.at[i], {"ctx": other})
        for i, (source, target) in enumerate(swaps)
    ]
    block_rows = tokens // count
    step_rows = 4 * block_rows
    mid = layers // 2
    near = (depth // mid) * mid
    order = [mid - near + (depth + step) % mid for step in range(mid)]
    order += [near + (depth + step) % mid for step in range(1, mid)] + [depth]
    asked = []
    for step in range(layers):
        span = rows(order[step] * step_rows, step_rows)
        slot = len(swaps) + step
        asked.append(
            remote(
                query_hbm.at[0, span],
                queries.at[span],
                ctx_send.at[slot],
                ctx_recv.at[slot],
                {"ctx": other, "hs": core_peer},
            )
        )

    @pl.when(helper)
    def _():
        for copy in outgoing[-1:] + outgoing[:-1] + asked:
            copy.start()

    def full_copy(source, index, slot, device):
        return remote(
            source,
            full.at[rows(index * shard, shard)],
            full_send.at[slot],
            full_recv.at[index],
            {"hs": device},
        )

    def arrived(index):
        block = full.at[rows(index * shard, shard)]
        remote(block, block, full_send.at[0], full_recv.at[index], {"hs": core_peer}).wait_recv()

    def held(index):
        return full.at[rows(index * shard, shard)]

    sends = [
        (depth < layers - 1, full_copy(weight_hbm, me, 0, me + 4)),
        (depth > 0, full_copy(weight_hbm, me, 1, me - 4)),
        (None, full_copy(weight_hbm, me, 2, row_peer)),
        (None, full_copy(weight_hbm, me, 3, core_peer)),
    ]

    for condition, copy in sends:
        guarded(condition, copy.start)

    for i in range(layers + 1):
        greet(ready.at[i])
        pl.semaphore_wait(ready.at[i], link_count)

    def relay(hop):
        for turn, (exists, onward) in enumerate(
            (
                (depth >= hop, depth < layers - 1),
                (depth + hop <= layers - 1, depth > 0),
            )
        ):
            index = me - 4 * hop if turn == 0 else me + 4 * hop
            slot = 4 + ((hop - 1) * 2 + turn) * 3
            next_device = me + 4 if turn == 0 else me - 4
            made = [
                (exists & onward, full_copy(held(index), index, slot, next_device)),
                (exists, full_copy(held(index), index, slot + 1, row_peer)),
                (exists, full_copy(held(index), index, slot + 2, core_peer)),
            ]
            pl.when(exists)(functools.partial(arrived, index))
            for condition, copy in made:
                guarded(condition, copy.start)
            sends.extend(made)

    crossed = []
    for step in range(layers):
        index = ((depth + step) % layers) * 4 + (1 - row) * 2 + core
        slot = 4 + 6 * (layers - 1) + step
        crossed.append((index, full_copy(held(index), index, slot, core_peer)))

    def cross():
        for index, copy in crossed:
            arrived(index)
            copy.start()

    def learn(start, rate, first):
        key_part = keys[rows(start, piece), :]
        rate_column = jnp.broadcast_to(rate, (128, piece)).T[:, :1]
        scaled_part = (rate_column * values[rows(start, piece), :].astype(jnp.float32)).astype(
            jnp.bfloat16
        )
        pre_gate = inner_cols(key_part, fast[0])
        pre_up = inner_cols(key_part, fast[1])
        sig_gate = jax.nn.sigmoid(pre_gate)
        act_gate = pre_gate * sig_gate
        hidden = (act_gate * pre_up).astype(jnp.bfloat16)
        back_hidden = jnp.dot(scaled_part, fast[2], preferred_element_type=jnp.float32)
        back_gate = (
            back_hidden * pre_up * sig_gate * (1.0 + pre_gate * (1.0 - sig_gate))
        ).astype(jnp.bfloat16)
        back_up = (back_hidden * act_gate).astype(jnp.bfloat16)
        terms = (
            inner_rows(back_gate, key_part),
            inner_rows(back_up, key_part),
            inner_rows(scaled_part, hidden),
        )
        for i, term in enumerate(terms):
            grads[i] = term if first else grads[i] + term

    handed = [
        remote(fresh.at[i], fresh.at[i], fresh_send.at[i], fresh_recv.at[i], {"hs": core_peer})
        for i in range(3)
    ]
    local[7].wait()
    gate = side[...].astype(jnp.float32)
    opened[...] = gate * jax.nn.sigmoid(gate)
    hops = list(range(1, layers))
    if hops:
        relay(hops.pop(0))

    @pl.when(owner)
    def _():
        for i in owned[:5]:
            local[i].wait()
        for copy in incoming[:3]:
            copy.wait_recv()
        for j in range(pieces):
            learn(ctx * tokens + j * piece, rate_ref[:, j * piece : (j + 1) * piece], j == 0)

    for j in range(pieces):
        if hops:
            relay(hops.pop(0))

        @pl.when(owner)
        def _():
            if j == 0:
                incoming[-1].wait_recv()
            incoming[3 + 2 * j].wait_recv()
            incoming[4 + 2 * j].wait_recv()
            learn(other * tokens + j * piece, rates[:, j * piece : (j + 1) * piece], False)

    for hop in hops:
        relay(hop)

    @pl.when(owner)
    def _():
        for i in range(3):
            fresh[i] = rescale_rows(fast[i], grads[i])
            handed[i].start()
        local[6].wait()

    @pl.when(helper)
    def _():
        cross()
        for copy in handed:
            copy.wait_recv()

    copies = []
    for step in range(1, layers + 1):
        target = order[step - 1]
        pl.when(helper)(asked[step - 1].wait_recv)
        query_part = queries[rows(target * step_rows, step_rows), :]
        query_gate = inner_cols(query_part, fresh[0])
        query_up = inner_cols(query_part, fresh[1])
        query_hidden = (query_gate * jax.nn.sigmoid(query_gate) * query_up).astype(jnp.bfloat16)
        head_part = inner_cols(query_hidden, fresh[2]).astype(jnp.bfloat16)
        heads[rows(target * step_rows, step_rows), :] = head_part
        for i in range(4):
            device = target * 4 + (inner + i) % 4
            source = heads.at[rows(device * block_rows, block_rows)]
            slot = len(copies)
            copy = remote(
                source,
                mixed.at[pair],
                head_send.at[slot],
                head_recv.at[pair],
                {"ctx": core, "hs": device},
            )
            condition = None
            if step == layers and i == 0:
                condition = helper

                @pl.when(owner)
                def _():
                    mixed[me] = source[...]

            guarded(condition, copy.start)
            copies.append((condition, copy))

    pl.when(owner)(cross)
    local[5].wait()
    for step in range(layers):
        for other_row in range(2):
            arrived(((depth + step) % layers) * 4 + ((row + other_row) % 2) * 2 + (1 - core))

    def head_arrived(index):
        remote(
            heads.at[pl.ds(0, block_rows)],
            mixed.at[index],
            head_send.at[0],
            head_recv.at[index],
            {"hs": core_peer},
        ).wait_recv()

    for step in range(1, count):
        head_arrived((me + step) % count)
    pl.when(helper)(functools.partial(head_arrived, me))

    for condition, copy in sends + copies:
        guarded(condition, copy.wait_send)
    for _, copy in crossed:
        copy.wait_send()

    @pl.when(helper)
    def _():
        for copy in outgoing + asked:
            copy.wait_send()

    @pl.when(owner)
    def _():
        for copy in handed:
            copy.wait_send()

    size = mixed.shape[2]
    head_count = side.shape[2] // size
    for seq in range(side.shape[1]):
        for head in range(head_count):
            columns = slice(head * size, (head + 1) * size)
            value = mixed[seq * head_count + head].astype(jnp.float32)
            square = jnp.mean(value * value, -1, keepdims=True)
            value = value * lax.rsqrt(square + epsilon) * gain_ref[:, columns]
            normed[seq * block_rows : (seq + 1) * block_rows, columns] = (
                value * opened[:, seq, columns]
            ).astype(jnp.bfloat16)
    result = jnp.dot(normed[...], full[...], preferred_element_type=jnp.float32)
    for seq in range(side.shape[1]):
        laid[:, seq, :] = result[seq * block_rows : (seq + 1) * block_rows]
    out_ref[...] = laid[...].astype(jnp.bfloat16)


def swapped_body(
    key_rows,
    value_rows,
    query_rows,
    step_rates,
    fast_gate,
    fast_up,
    fast_down,
    out_gain,
    gate_input,
    out_weight,
):
    layers = lax.axis_size("hs") // 4
    count = 4 * layers
    pieces = 2
    tokens, size = key_rows.shape[1:]
    hidden_size = 2 * fast_gate.shape[1]
    block_rows, seq_count, width = gate_input.shape
    columns = out_weight.shape[1]
    anywhere = pl.BlockSpec(memory_space=pl.ANY)
    inside = pl.BlockSpec(memory_space=pltpu.VMEM)
    half = jnp.bfloat16
    return pl.pallas_call(
        functools.partial(layer_kernel, layers, pieces),
        out_shape=jax.ShapeDtypeStruct((block_rows, seq_count, columns), half),
        in_specs=[anywhere] * 8 + [inside] * 2,
        out_specs=inside,
        scratch_shapes=[
            pltpu.VMEM((3, hidden_size, size), half),
            pltpu.VMEM((3, hidden_size, size), half),
            pltpu.VMEM((2 * tokens, size), half),
            pltpu.VMEM((2 * tokens, size), half),
            pltpu.VMEM((1, tokens), jnp.float32),
            pltpu.VMEM((tokens, size), half),
            pltpu.VMEM((block_rows, seq_count, width), half),
            pltpu.VMEM((block_rows, seq_count, width), jnp.float32),
            pltpu.VMEM((width, columns), half),
            pltpu.VMEM((3, hidden_size, size), jnp.float32),
            pltpu.VMEM((tokens, size), half),
            pltpu.VMEM((count, block_rows, size), half),
            pltpu.VMEM((seq_count * block_rows, width), half),
            pltpu.VMEM((block_rows, seq_count, columns), jnp.float32),
            pltpu.SemaphoreType.DMA((8,)),
            pltpu.SemaphoreType.DMA((4 + 2 * pieces + layers,)),
            pltpu.SemaphoreType.DMA((4 + 2 * pieces + layers,)),
            pltpu.SemaphoreType.DMA((4 + 6 * (layers - 1) + layers,)),
            pltpu.SemaphoreType.DMA((count,)),
            pltpu.SemaphoreType.DMA((count,)),
            pltpu.SemaphoreType.DMA((count,)),
            pltpu.SemaphoreType.DMA((3,)),
            pltpu.SemaphoreType.DMA((3,)),
            pltpu.SemaphoreType.REGULAR((layers + 1,)),
        ],
        compiler_params=pltpu.CompilerParams(
            collective_id=0, has_side_effects=True, vmem_limit_bytes=60 * 1024 * 1024
        ),
    )(
        fast_gate,
        fast_up,
        fast_down,
        key_rows,
        value_rows,
        query_rows,
        gate_input,
        out_weight,
        step_rates,
        out_gain[None],
    )

def solution(mesh):
    def step(*arrays):
        paired = mesh.shape["ctx"] == 2 and mesh.shape["hs"] % 8 == 0
        paired = paired and arrays[0].shape[0] == 1
        return (swapped_body if paired else body)(*arrays)

    return jax.shard_map(
        step,
        mesh=mesh,
        in_specs=(
            P("hs", "ctx", None),
            P("hs", "ctx", None),
            P("hs", "ctx", None),
            P("hs", "ctx"),
            P("hs", "ctx", None),
            P("hs", "ctx", None),
            P("hs", "ctx", None),
            P(),
            P(("ctx", "hs"), None, None),
            P("hs", None),
        ),
        out_specs=P(("ctx", "hs"), None, None),
        check_vma=False,
    )
```

```python
import functools

import jax
import jax.numpy as jnp
from jax import lax
from jax.experimental import pallas as pl
from jax.experimental.pallas import tpu as pltpu
from jax.sharding import PartitionSpec as P

epsilon = 1e-06


def rescale_rows(weight, update):
    base = weight.astype(jnp.float32)
    moved = base + update
    factor = jnp.sqrt(jnp.mean(base * base, -1, keepdims=True) + epsilon) / jnp.sqrt(
        jnp.mean(moved * moved, -1, keepdims=True) + epsilon
    )
    return (moved * factor).astype(jnp.bfloat16)


def inner_rows(left, right):
    return lax.dot_general(
        left, right, (((0,), (0,)), ((), ())), preferred_element_type=jnp.float32
    )


def body(
    key_rows,
    value_rows,
    query_rows,
    step_rates,
    fast_gate,
    fast_up,
    fast_down,
    out_gain,
    gate_input,
    out_weight,
):
    key_row = key_rows[0]
    value_row = value_rows[0]
    query_row = query_rows[0]
    rate_row = step_rates[0]
    whole_gate, whole_up, whole_down = (
        lax.all_gather(fast_gate, "ctx", axis=1, tiled=True),
        lax.all_gather(fast_up, "ctx", axis=1, tiled=True),
        lax.all_gather(fast_down, "ctx", axis=1, tiled=True),
    )
    gate_fast = whole_gate[0]
    up_fast = whole_up[0]
    down_fast = whole_down[0]
    pre_gate = jnp.dot(key_row, gate_fast.T, preferred_element_type=jnp.float32)
    pre_up = jnp.dot(key_row, up_fast.T, preferred_element_type=jnp.float32)
    sig_gate = jax.nn.sigmoid(pre_gate)
    act_gate = pre_gate * sig_gate
    hidden = (act_gate * pre_up).astype(jnp.bfloat16)
    scaled = (rate_row[:, None] * value_row.astype(jnp.float32)).astype(jnp.bfloat16)
    grad_down = inner_rows(scaled, hidden)
    back_hidden = jnp.dot(scaled, down_fast, preferred_element_type=jnp.float32)
    back_gate = (back_hidden * pre_up * sig_gate * (1.0 + pre_gate * (1.0 - sig_gate))).astype(
        jnp.bfloat16
    )
    back_up = (back_hidden * act_gate).astype(jnp.bfloat16)
    grad_gate = inner_rows(back_gate, key_row)
    grad_up = inner_rows(back_up, key_row)
    grad_gate, grad_up, grad_down = (
        lax.psum_scatter(grad_gate, "ctx", scatter_dimension=0, tiled=True),
        lax.psum_scatter(grad_up, "ctx", scatter_dimension=0, tiled=True),
        lax.psum_scatter(grad_down, "ctx", scatter_dimension=0, tiled=True),
    )
    part_gate = rescale_rows(fast_gate[0], grad_gate)
    part_up = rescale_rows(fast_up[0], grad_up)
    part_down = rescale_rows(fast_down[0], grad_down)
    new_gate, new_up, new_down = (
        lax.all_gather(part_gate, "ctx", axis=0, tiled=True),
        lax.all_gather(part_up, "ctx", axis=0, tiled=True),
        lax.all_gather(part_down, "ctx", axis=0, tiled=True),
    )
    query_gate = jnp.dot(query_row, new_gate.T, preferred_element_type=jnp.float32)
    query_up = jnp.dot(query_row, new_up.T, preferred_element_type=jnp.float32)
    query_hidden = (jax.nn.silu(query_gate) * query_up).astype(jnp.bfloat16)
    head_out = jnp.dot(query_hidden, new_down.T, preferred_element_type=jnp.float32).astype(
        jnp.bfloat16
    )
    width_hs = lax.axis_size("hs")
    head_size = head_out.shape[1]
    token_count = head_out.shape[0] // width_hs
    blocks = head_out.reshape(width_hs, token_count, head_size)
    moved = lax.all_to_all(blocks, "hs", split_axis=0, concat_axis=2, tiled=True)
    seq_count = gate_input.shape[1]
    model_width = gate_input.shape[2]
    head_count = model_width // head_size
    mixed = moved.reshape(token_count, seq_count, head_count, head_size).astype(jnp.float32)
    square = jnp.mean(mixed * mixed, -1, keepdims=True)
    scaled_heads = mixed * lax.rsqrt(square + epsilon) * out_gain.reshape(head_count, head_size)
    normed = (
        scaled_heads.reshape(token_count, seq_count, model_width)
        * jax.nn.silu(gate_input.astype(jnp.float32))
    ).astype(jnp.bfloat16)
    flat_rows = normed.reshape(token_count * seq_count, model_width)
    out_cols = out_weight.shape[1]
    full_weight = lax.all_gather(out_weight, "hs", axis=0, tiled=True)
    result = jnp.dot(flat_rows, full_weight, preferred_element_type=jnp.float32)
    return result.astype(jnp.bfloat16).reshape(token_count, seq_count, out_cols)


MESH = pl.DeviceIdType.MESH


def inner_cols(left, right):
    return lax.dot_general(
        left, right, (((1,), (1,)), ((), ())), preferred_element_type=jnp.float32
    )


def layer_kernel(
    layers,
    pieces,
    gate_hbm,
    up_hbm,
    down_hbm,
    key_hbm,
    value_hbm,
    query_hbm,
    side_hbm,
    weight_hbm,
    rate_hbm,
    gain_hbm,
    out_ref,
    fast,
    fresh,
    keys,
    values,
    rates,
    queries,
    gain,
    side,
    moved,
    gates,
    full,
    grads,
    heads,
    mixed,
    normed,
    outs,
    landed,
    laid,
    local_sem,
    ctx_send,
    ctx_recv,
    full_send,
    full_recv,
    gate_send,
    gate_recv,
    head_send,
    head_recv,
    out_send,
    out_recv,
    ready,
):
    ctx = lax.axis_index("ctx")
    me = lax.axis_index("hs")
    other = 1 - ctx
    count = 4 * layers
    last = layers - 1
    depth, inner = me // 4, me % 4
    row, core = inner // 2, inner % 2
    row_peer = depth * 4 + (1 - row) * 2 + core
    core_peer = depth * 4 + row * 2 + (1 - core)
    owner = core == ctx
    helper = core != ctx
    part = gate_hbm.shape[1]
    tokens = key_hbm.shape[1]
    piece = tokens // pieces
    shard = weight_hbm.shape[0]
    block_rows = tokens // count
    step_rows = 4 * block_rows
    seq_count = side.shape[1]
    size = key_hbm.shape[2]
    head_count = side.shape[2] // size

    def remote(source, target, send, recv, device):
        return pltpu.make_async_remote_copy(
            src_ref=source,
            dst_ref=target,
            send_sem=send,
            recv_sem=recv,
            device_id=device,
            device_id_type=MESH,
        )

    def rows(start, size):
        return pl.ds(pl.multiple_of(start, size), size)

    def guarded(condition, action):
        if condition is None:
            action()
        else:
            pl.when(condition)(action)

    links = [
        (None, {"ctx": other}),
        (None, {"hs": row_peer}),
        (None, {"hs": core_peer}),
        (depth < last, {"hs": me + 4}),
        (depth > 0, {"hs": me - 4}),
    ]
    link_count = 3 + jnp.where(depth < last, 1, 0) + jnp.where(depth > 0, 1, 0)

    def greet(semaphore):
        for condition, device in links:
            guarded(
                condition,
                functools.partial(
                    pl.semaphore_signal, semaphore, inc=1, device_id=device, device_id_type=MESH
                ),
            )

    barrier = pltpu.get_barrier_semaphore()
    greet(barrier)

    weights = (gate_hbm, up_hbm, down_hbm)
    near = rows(ctx * tokens, tokens)
    local = []
    for i, source in enumerate(weights):
        local.append((source.at[0], fast.at[i, rows(ctx * part, part)]))
    local.append((key_hbm.at[0], keys.at[near]))
    local.append((value_hbm.at[0], values.at[near]))
    local.append((query_hbm.at[0], queries.at[near]))
    local.append((rate_hbm, rates.at[ctx]))
    local.append((side_hbm, side))
    local.append((weight_hbm, full.at[rows(me * shard, shard)]))
    local.append((gain_hbm, gain))
    local = [
        pltpu.make_async_copy(source, target, local_sem.at[i])
        for i, (source, target) in enumerate(local)
    ]
    owned = local[:7]

    @pl.when(owner)
    def _():
        for copy in owned:
            copy.start()

    for copy in local[7:]:
        copy.start()
    pl.semaphore_wait(barrier, link_count)

    mid = layers // 2
    side_half = (depth // mid) * mid
    order = [mid - side_half + (depth + step) % mid for step in range(mid)]
    order += [side_half + (depth + step) % mid for step in range(1, mid)] + [depth]

    swaps = [(rate_hbm, lambda who: rates.at[who])]
    for i, source in enumerate(weights):
        swaps.append((source.at[0], lambda who, i=i: fast.at[i, rows(who * part, part)]))
    for j in range(pieces):
        for source, target in ((key_hbm.at[0], keys), (value_hbm.at[0], values)):
            swaps.append(
                (
                    source.at[pl.ds(j * piece, piece)],
                    lambda who, target=target, j=j: target.at[
                        rows(who * tokens + j * piece, piece)
                    ],
                )
            )
    for step in range(layers):
        swaps.append(
            (
                query_hbm.at[0, rows(order[step] * step_rows, step_rows)],
                lambda who, step=step: queries.at[
                    rows(who * tokens + order[step] * step_rows, step_rows)
                ],
            )
        )
    outgoing = [
        remote(source, target(ctx), ctx_send.at[i], ctx_recv.at[i], {"ctx": other})
        for i, (source, target) in enumerate(swaps)
    ]
    incoming = [
        remote(source, target(other), ctx_send.at[i], ctx_recv.at[i], {"ctx": other})
        for i, (source, target) in enumerate(swaps)
    ]
    asked = incoming[-layers:]

    def held(index):
        return full.at[rows(index * shard, shard)]

    used = []

    def full_copy(source, index, device):
        slot = len(used)
        used.append(slot)
        return remote(source, held(index), full_send.at[slot], full_recv.at[index], {"hs": device})

    def arrived(index):
        block = held(index)
        remote(block, block, full_send.at[0], full_recv.at[index], {"hs": core_peer}).wait_recv()

    def start_all(made):
        for condition, copy in made:
            guarded(condition, copy.start)

    first_sends = [
        (None, full_copy(weight_hbm, me, core_peer)),
        (depth < last, full_copy(weight_hbm, me, me + 4)),
        (depth > 0, full_copy(weight_hbm, me, me - 4)),
        (None, full_copy(weight_hbm, me, row_peer)),
    ]
    second_sends = [
        (depth < last, full_copy(held(core_peer), core_peer, me + 4)),
        (depth > 0, full_copy(held(core_peer), core_peer, me - 4)),
        (None, full_copy(held(core_peer), core_peer, row_peer)),
    ]
    relays = []
    for hop in range(1, layers):
        for base in (me, core_peer):
            for upward in (True, False):
                exists = depth >= hop if upward else depth + hop <= last
                onward = depth < last if upward else depth > 0
                index = base - 4 * hop if upward else base + 4 * hop
                next_device = me + 4 if upward else me - 4
                made = [
                    (exists & onward, full_copy(held(index), index, next_device)),
                    (exists, full_copy(held(index), index, row_peer)),
                    (exists, full_copy(held(index), index, core_peer)),
                ]
                relays.append((hop, exists, index, made))
    crossed = []
    for step in range(layers):
        for base in (row_peer, depth * 4 + (1 - row) * 2 + (1 - core)):
            index = (base + 4 * step) % count
            crossed.append((index, full_copy(held(index), index, core_peer)))

    own_copy = remote(
        weight_hbm, held(me), full_send.at[0], full_recv.at[me], {"hs": core_peer}
    )

    @pl.when(owner)
    def _():
        own_copy.start()

    @pl.when(helper)
    def _():
        for copy in outgoing:
            copy.start()
        start_all(first_sends)

    for i in range(max(2, layers - 2)):
        greet(ready.at[i])
        pl.semaphore_wait(ready.at[i], link_count)

    @pl.when(helper)
    def _():
        arrived(core_peer)
        start_all(second_sends)

    local[7].wait()
    spread = side[...].astype(jnp.float32)
    for seq in range(seq_count):
        moved[seq] = spread[:, seq, :].astype(jnp.bfloat16)
    gate_copies = [
        remote(
            moved.at[order[step]],
            gates.at[depth],
            gate_send.at[step],
            gate_recv.at[depth],
            {"hs": order[step] * 4 + inner},
        )
        for step in range(last)
    ]

    @pl.when(helper)
    def _():
        opened_hop = max(1, layers - 2)
        for position, (hop, exists, index, made) in enumerate(relays):
            pl.when(exists)(functools.partial(arrived, index))
            start_all(made)
            if hop == opened_hop and position + 1 == 4 * opened_hop:
                for copy in gate_copies:
                    copy.start()
        for index, copy in crossed:
            arrived(index)
            copy.start()

    def learn(start, rate, first):
        key_part = keys[rows(start, piece), :]
        rate_column = jnp.broadcast_to(rate, (128, piece)).T[:, :1]
        scaled_part = (rate_column * values[rows(start, piece), :].astype(jnp.float32)).astype(
            jnp.bfloat16
        )
        pre_gate = inner_cols(key_part, fast[0])
        pre_up = inner_cols(key_part, fast[1])
        sig_gate = jax.nn.sigmoid(pre_gate)
        act_gate = pre_gate * sig_gate
        hidden = (act_gate * pre_up).astype(jnp.bfloat16)
        back_hidden = jnp.dot(scaled_part, fast[2], preferred_element_type=jnp.float32)
        back_gate = (
            back_hidden * pre_up * sig_gate * (1.0 + pre_gate * (1.0 - sig_gate))
        ).astype(jnp.bfloat16)
        back_up = (back_hidden * act_gate).astype(jnp.bfloat16)
        terms = (
            inner_rows(back_gate, key_part),
            inner_rows(back_up, key_part),
            inner_rows(scaled_part, hidden),
        )
        for i, term in enumerate(terms):
            grads[i] = term if first else grads[i] + term

    head_copies = {}
    for half in (other, ctx):
        for step in range(layers):
            start = half * tokens + order[step] * step_rows
            for i in range(3 if half is ctx else 4):
                place = (inner + 1 + i) % 4
                head_copies[half is ctx, step, i] = remote(
                    heads.at[rows(start + place * block_rows, block_rows)],
                    mixed.at[order[step], row * 2 + ctx],
                    head_send.at[len(head_copies)],
                    head_recv.at[order[step], row * 2 + ctx],
                    {"ctx": half, "hs": depth * 4 + place},
                )

    def answer(half, step):
        target = order[step]
        start = half * tokens + target * step_rows
        query_part = queries[rows(start, step_rows), :]
        query_gate = inner_cols(query_part, fresh[0])
        query_up = inner_cols(query_part, fresh[1])
        query_hidden = (query_gate * jax.nn.sigmoid(query_gate) * query_up).astype(jnp.bfloat16)
        heads[rows(start, step_rows), :] = inner_cols(query_hidden, fresh[2]).astype(jnp.bfloat16)
        for i in range(4):
            if half is ctx and i == 3:
                mixed[target, row * 2 + ctx] = heads[
                    rows(start + inner * block_rows, block_rows), :
                ]
            else:
                head_copies[half is ctx, step, i].start()

    @pl.when(owner)
    def _():
        for i in (0, 1, 2, 3, 4, 6):
            local[i].wait()
        for copy in gate_copies:
            copy.start()
        for copy in incoming[1:4]:
            copy.wait_recv()
        for j in range(pieces):
            learn(ctx * tokens + j * piece, rates[ctx, :, j * piece : (j + 1) * piece], j == 0)
        incoming[0].wait_recv()
        for j in range(pieces):
            incoming[4 + 2 * j].wait_recv()
            incoming[5 + 2 * j].wait_recv()
            learn(
                other * tokens + j * piece, rates[other, :, j * piece : (j + 1) * piece], False
            )
        for i in range(3):
            fresh[i] = rescale_rows(fast[i], grads[i])
        local[5].wait()
        for step in range(layers):
            asked[step].wait_recv()
            answer(other, step)
            answer(ctx, step)
        for step in range(1, count):
            arrived((me + step) % count)

    local[8].wait()
    local[9].wait()

    def wait_head(target, slot):
        block = mixed.at[target, slot]
        remote(
            block, block, head_send.at[0], head_recv.at[target, slot], {"hs": core_peer}
        ).wait_recv()

    out_copies = []
    for step in range(layers):
        target = order[step]
        for i in range(3):
            wait_head(target, (row * 2 + ctx + 1 + i) % 4)
        pl.when(helper)(functools.partial(wait_head, target, row * 2 + ctx))
        if step < last:
            block = gates.at[target]
            remote(
                block, block, gate_send.at[0], gate_recv.at[target], {"hs": core_peer}
            ).wait_recv()
            opened = gates[target]
        else:
            opened = moved[depth]
        opened = opened.astype(jnp.float32)
        opened = opened * jax.nn.sigmoid(opened)
        for head in range(head_count):
            columns = slice(head * size, (head + 1) * size)
            value = mixed[target, head].astype(jnp.float32)
            square = jnp.mean(value * value, -1, keepdims=True)
            value = value * lax.rsqrt(square + epsilon) * gain[:, columns]
            normed[step, :, columns] = (value * opened[:, columns]).astype(jnp.bfloat16)
        result = jnp.dot(normed[step], full[...], preferred_element_type=jnp.float32)
        if step < last:
            outs[step] = result.astype(jnp.bfloat16)
            copy = remote(
                outs.at[step],
                landed.at[depth],
                out_send.at[step],
                out_recv.at[depth],
                {"hs": target * 4 + inner},
            )
            copy.start()
            out_copies.append(copy)
        else:
            landed[depth] = result.astype(jnp.bfloat16)

    @pl.when(owner)
    def _():
        own_copy.wait_send()
        for copy in head_copies.values():
            copy.wait_send()

    @pl.when(helper)
    def _():
        for copy in outgoing:
            copy.wait_send()
        for condition, copy in first_sends + second_sends:
            guarded(condition, copy.wait_send)
        for _, _, _, made in relays:
            for condition, copy in made:
                guarded(condition, copy.wait_send)
        for _, copy in crossed:
            copy.wait_send()

    for copy in gate_copies:
        copy.wait_send()
    for step in range(1, layers):
        source = (depth + step) % layers
        block = landed.at[source]
        remote(block, block, out_send.at[0], out_recv.at[source], {"hs": core_peer}).wait_recv()
    for copy in out_copies:
        copy.wait_send()
    for seq in range(seq_count):
        laid[:, seq, :] = landed[seq].astype(jnp.float32)
    out_ref[...] = laid[...].astype(jnp.bfloat16)


def swapped_body(
    key_rows,
    value_rows,
    query_rows,
    step_rates,
    fast_gate,
    fast_up,
    fast_down,
    out_gain,
    gate_input,
    out_weight,
):
    layers = lax.axis_size("hs") // 4
    count = 4 * layers
    pieces = 2
    tokens, size = key_rows.shape[1:]
    hidden_size = 2 * fast_gate.shape[1]
    block_rows, seq_count, width = gate_input.shape
    columns = out_weight.shape[1]
    anywhere = pl.BlockSpec(memory_space=pl.ANY)
    inside = pl.BlockSpec(memory_space=pltpu.VMEM)
    half = jnp.bfloat16
    dma = pltpu.SemaphoreType.DMA
    swaps = 4 + 2 * pieces + layers
    return pl.pallas_call(
        functools.partial(layer_kernel, layers, pieces),
        out_shape=jax.ShapeDtypeStruct((block_rows, seq_count, columns), half),
        in_specs=[anywhere] * 10,
        out_specs=inside,
        scratch_shapes=[
            pltpu.VMEM((3, hidden_size, size), half),
            pltpu.VMEM((3, hidden_size, size), half),
            pltpu.VMEM((2 * tokens, size), half),
            pltpu.VMEM((2 * tokens, size), half),
            pltpu.VMEM((2, 1, tokens), jnp.float32),
            pltpu.VMEM((2 * tokens, size), half),
            pltpu.VMEM((1, width), jnp.float32),
            pltpu.VMEM((block_rows, seq_count, width), half),
            pltpu.VMEM((seq_count, block_rows, width), half),
            pltpu.VMEM((layers, block_rows, width), half),
            pltpu.VMEM((width, columns), half),
            pltpu.VMEM((3, hidden_size, size), jnp.float32),
            pltpu.VMEM((2 * tokens, size), half),
            pltpu.VMEM((layers, 4, block_rows, size), half),
            pltpu.VMEM((layers, block_rows, width), half),
            pltpu.VMEM((layers, block_rows, columns), half),
            pltpu.VMEM((seq_count, block_rows, columns), half),
            pltpu.VMEM((block_rows, seq_count, columns), jnp.float32),
            dma((10,)),
            dma((swaps,)),
            dma((swaps,)),
            dma((7 + 12 * (layers - 1) + 2 * layers,)),
            dma((count,)),
            dma((layers,)),
            dma((layers,)),
            dma((8 * layers,)),
            dma((layers, 4)),
            dma((layers,)),
            dma((layers,)),
            pltpu.SemaphoreType.REGULAR((max(2, layers - 2),)),
        ],
        compiler_params=pltpu.CompilerParams(
            collective_id=0, has_side_effects=True, vmem_limit_bytes=60 * 1024 * 1024
        ),
    )(
        fast_gate,
        fast_up,
        fast_down,
        key_rows,
        value_rows,
        query_rows,
        gate_input,
        out_weight,
        step_rates,
        out_gain[None],
    )


def solution(mesh):
    def step(*arrays):
        paired = mesh.shape["ctx"] == 2 and mesh.shape["hs"] % 8 == 0
        paired = paired and arrays[0].shape[0] == 1
        paired = paired and arrays[8].shape[1] == mesh.shape["hs"] // 4
        paired = paired and arrays[8].shape[2] == 4 * arrays[0].shape[2]
        return (swapped_body if paired else body)(*arrays)

    return jax.shard_map(
        step,
        mesh=mesh,
        in_specs=(
            P("hs", "ctx", None),
            P("hs", "ctx", None),
            P("hs", "ctx", None),
            P("hs", "ctx"),
            P("hs", "ctx", None),
            P("hs", "ctx", None),
            P("hs", "ctx", None),
            P(),
            P(("ctx", "hs"), None, None),
            P("hs", None),
        ),
        out_specs=P(("ctx", "hs"), None, None),
        check_vma=False,
    )
```

```python
import functools

import jax
import jax.numpy as jnp
from jax import lax
from jax.experimental import pallas as pl
from jax.experimental.pallas import tpu as pltpu
from jax.sharding import PartitionSpec as P

epsilon = 1e-06


def rescale_rows(weight, update):
    base = weight.astype(jnp.float32)
    moved = base + update
    factor = jnp.sqrt(jnp.mean(base * base, -1, keepdims=True) + epsilon) / jnp.sqrt(
        jnp.mean(moved * moved, -1, keepdims=True) + epsilon
    )
    return (moved * factor).astype(jnp.bfloat16)


def inner_rows(left, right):
    return lax.dot_general(
        left, right, (((0,), (0,)), ((), ())), preferred_element_type=jnp.float32
    )


def body(
    key_rows,
    value_rows,
    query_rows,
    step_rates,
    fast_gate,
    fast_up,
    fast_down,
    out_gain,
    gate_input,
    out_weight,
):
    key_row = key_rows[0]
    value_row = value_rows[0]
    query_row = query_rows[0]
    rate_row = step_rates[0]
    whole_gate, whole_up, whole_down = (
        lax.all_gather(fast_gate, "ctx", axis=1, tiled=True),
        lax.all_gather(fast_up, "ctx", axis=1, tiled=True),
        lax.all_gather(fast_down, "ctx", axis=1, tiled=True),
    )
    gate_fast = whole_gate[0]
    up_fast = whole_up[0]
    down_fast = whole_down[0]
    pre_gate = jnp.dot(key_row, gate_fast.T, preferred_element_type=jnp.float32)
    pre_up = jnp.dot(key_row, up_fast.T, preferred_element_type=jnp.float32)
    sig_gate = jax.nn.sigmoid(pre_gate)
    act_gate = pre_gate * sig_gate
    hidden = (act_gate * pre_up).astype(jnp.bfloat16)
    scaled = (rate_row[:, None] * value_row.astype(jnp.float32)).astype(jnp.bfloat16)
    grad_down = inner_rows(scaled, hidden)
    back_hidden = jnp.dot(scaled, down_fast, preferred_element_type=jnp.float32)
    back_gate = (back_hidden * pre_up * sig_gate * (1.0 + pre_gate * (1.0 - sig_gate))).astype(
        jnp.bfloat16
    )
    back_up = (back_hidden * act_gate).astype(jnp.bfloat16)
    grad_gate = inner_rows(back_gate, key_row)
    grad_up = inner_rows(back_up, key_row)
    grad_gate, grad_up, grad_down = (
        lax.psum_scatter(grad_gate, "ctx", scatter_dimension=0, tiled=True),
        lax.psum_scatter(grad_up, "ctx", scatter_dimension=0, tiled=True),
        lax.psum_scatter(grad_down, "ctx", scatter_dimension=0, tiled=True),
    )
    part_gate = rescale_rows(fast_gate[0], grad_gate)
    part_up = rescale_rows(fast_up[0], grad_up)
    part_down = rescale_rows(fast_down[0], grad_down)
    new_gate, new_up, new_down = (
        lax.all_gather(part_gate, "ctx", axis=0, tiled=True),
        lax.all_gather(part_up, "ctx", axis=0, tiled=True),
        lax.all_gather(part_down, "ctx", axis=0, tiled=True),
    )
    query_gate = jnp.dot(query_row, new_gate.T, preferred_element_type=jnp.float32)
    query_up = jnp.dot(query_row, new_up.T, preferred_element_type=jnp.float32)
    query_hidden = (jax.nn.silu(query_gate) * query_up).astype(jnp.bfloat16)
    head_out = jnp.dot(query_hidden, new_down.T, preferred_element_type=jnp.float32).astype(
        jnp.bfloat16
    )
    width_hs = lax.axis_size("hs")
    head_size = head_out.shape[1]
    token_count = head_out.shape[0] // width_hs
    blocks = head_out.reshape(width_hs, token_count, head_size)
    moved = lax.all_to_all(blocks, "hs", split_axis=0, concat_axis=2, tiled=True)
    seq_count = gate_input.shape[1]
    model_width = gate_input.shape[2]
    head_count = model_width // head_size
    mixed = moved.reshape(token_count, seq_count, head_count, head_size).astype(jnp.float32)
    square = jnp.mean(mixed * mixed, -1, keepdims=True)
    scaled_heads = mixed * lax.rsqrt(square + epsilon) * out_gain.reshape(head_count, head_size)
    normed = (
        scaled_heads.reshape(token_count, seq_count, model_width)
        * jax.nn.silu(gate_input.astype(jnp.float32))
    ).astype(jnp.bfloat16)
    flat_rows = normed.reshape(token_count * seq_count, model_width)
    out_cols = out_weight.shape[1]
    full_weight = lax.all_gather(out_weight, "hs", axis=0, tiled=True)
    result = jnp.dot(flat_rows, full_weight, preferred_element_type=jnp.float32)
    return result.astype(jnp.bfloat16).reshape(token_count, seq_count, out_cols)


MESH = pl.DeviceIdType.MESH


def inner_cols(left, right):
    return lax.dot_general(
        left, right, (((1,), (1,)), ((), ())), preferred_element_type=jnp.float32
    )


def layer_kernel(
    layers,
    pieces,
    gate_hbm,
    up_hbm,
    down_hbm,
    key_hbm,
    value_hbm,
    query_hbm,
    side_hbm,
    weight_hbm,
    rate_hbm,
    gain_hbm,
    out_ref,
    fast,
    fresh,
    keys,
    values,
    rates,
    queries,
    gain,
    side,
    moved,
    gates,
    full,
    grads,
    heads,
    mixed,
    normed,
    outs,
    local_sem,
    ctx_send,
    ctx_recv,
    full_send,
    full_recv,
    gate_send,
    gate_recv,
    head_send,
    head_recv,
    out_send,
    out_recv,
    ready,
):
    ctx = lax.axis_index("ctx")
    me = lax.axis_index("hs")
    other = 1 - ctx
    count = 4 * layers
    last = layers - 1
    depth, inner = me // 4, me % 4
    row, core = inner // 2, inner % 2
    row_peer = depth * 4 + (1 - row) * 2 + core
    core_peer = depth * 4 + row * 2 + (1 - core)
    owner = core == ctx
    helper = core != ctx
    part = gate_hbm.shape[1]
    tokens = key_hbm.shape[1]
    piece = tokens // pieces
    shard = weight_hbm.shape[0]
    block_rows = tokens // count
    step_rows = 4 * block_rows
    seq_count = side.shape[1]
    size = key_hbm.shape[2]
    head_count = side.shape[2] // size

    def remote(source, target, send, recv, device):
        return pltpu.make_async_remote_copy(
            src_ref=source,
            dst_ref=target,
            send_sem=send,
            recv_sem=recv,
            device_id=device,
            device_id_type=MESH,
        )

    def rows(start, size):
        return pl.ds(pl.multiple_of(start, size), size)

    def drain(block, semaphore):
        pltpu.make_async_copy(block, block, semaphore).wait()

    def guarded(condition, action):
        if condition is None:
            action()
        else:
            pl.when(condition)(action)

    links = [
        (None, {"ctx": other}),
        (None, {"hs": row_peer}),
        (None, {"hs": core_peer}),
        (depth < last, {"hs": me + 4}),
        (depth > 0, {"hs": me - 4}),
    ]
    link_count = 3 + jnp.where(depth < last, 1, 0) + jnp.where(depth > 0, 1, 0)

    def greet(semaphore):
        for condition, device in links:
            guarded(
                condition,
                functools.partial(
                    pl.semaphore_signal, semaphore, inc=1, device_id=device, device_id_type=MESH
                ),
            )

    barrier = pltpu.get_barrier_semaphore()
    greet(barrier)

    weights = (gate_hbm, up_hbm, down_hbm)
    near = rows(ctx * tokens, tokens)
    owned = [
        pltpu.make_async_copy(source, target, local_sem.at[0])
        for source, target in [
            (source.at[0], fast.at[i, rows(ctx * part, part)])
            for i, source in enumerate(weights)
        ]
        + [
            (source.at[0], target.at[near])
            for source, target in ((key_hbm, keys), (value_hbm, values), (query_hbm, queries))
        ]
    ]
    own_rates = pltpu.make_async_copy(rate_hbm, rates.at[ctx], local_sem.at[1])
    side_copy = pltpu.make_async_copy(side_hbm, side, local_sem.at[2])
    own_shard = pltpu.make_async_copy(
        weight_hbm, full.at[rows(me * shard, shard)], local_sem.at[3]
    )
    gain_copy = pltpu.make_async_copy(gain_hbm, gain, local_sem.at[4])

    @pl.when(owner)
    def _():
        for copy in owned:
            copy.start()
        own_rates.start()

    for copy in (side_copy, own_shard, gain_copy):
        copy.start()
    pl.semaphore_wait(barrier, link_count)

    mid = layers // 2
    side_half = (depth // mid) * mid
    order = [mid - side_half + (depth + step) % mid for step in range(mid)]
    order += [side_half + (depth + step) % mid for step in range(1, mid)] + [depth]

    swaps = [(rate_hbm, lambda who: rates.at[who])]
    for i, source in enumerate(weights):
        swaps.append((source.at[0], lambda who, i=i: fast.at[i, rows(who * part, part)]))
    for j in range(pieces):
        for source, target in ((key_hbm.at[0], keys), (value_hbm.at[0], values)):
            swaps.append(
                (
                    source.at[pl.ds(j * piece, piece)],
                    lambda who, target=target, j=j: target.at[
                        rows(who * tokens + j * piece, piece)
                    ],
                )
            )
    for step in range(layers):
        swaps.append(
            (
                query_hbm.at[0, rows(order[step] * step_rows, step_rows)],
                lambda who, step=step: queries.at[
                    rows(who * tokens + order[step] * step_rows, step_rows)
                ],
            )
        )
    arrivals = [0, 1, 1, 1]
    arrivals += [2 + j for j in range(pieces) for _ in range(2)]
    arrivals += [2 + pieces + step for step in range(layers)]
    outgoing = [
        remote(
            source,
            target(ctx),
            ctx_send.at[0 if i == 0 else 1],
            ctx_recv.at[arrivals[i]],
            {"ctx": other},
        )
        for i, (source, target) in enumerate(swaps)
    ]
    def lines(count):
        return full.at[pl.ds(0, count * size // full.shape[1])]

    def held(index):
        return full.at[rows(index * shard, shard)]

    def full_copy(source, index, way, device):
        return remote(source, held(index), full_send.at[way], full_recv.at[index], {"hs": device})

    def arrived(index):
        block = held(index)
        remote(block, block, full_send.at[0], full_recv.at[index], {"hs": core_peer}).wait_recv()

    def start_all(made):
        for condition, copy in made:
            guarded(condition, copy.start)

    first_sends = [
        (None, full_copy(weight_hbm, me, 3, core_peer)),
        (depth < last, full_copy(weight_hbm, me, 0, me + 4)),
        (depth > 0, full_copy(weight_hbm, me, 1, me - 4)),
        (None, full_copy(weight_hbm, me, 2, row_peer)),
    ]
    second_sends = [
        (depth < last, full_copy(held(core_peer), core_peer, 0, me + 4)),
        (depth > 0, full_copy(held(core_peer), core_peer, 1, me - 4)),
        (None, full_copy(held(core_peer), core_peer, 2, row_peer)),
    ]
    relays = []
    for hop in range(1, layers):
        for base in (me, core_peer):
            for upward in (True, False):
                exists = depth >= hop if upward else depth + hop <= last
                onward = depth < last if upward else depth > 0
                index = base - 4 * hop if upward else base + 4 * hop
                next_device = me + 4 if upward else me - 4
                made = [
                    (exists & onward, full_copy(held(index), index, 0 if upward else 1, next_device)),
                    (exists, full_copy(held(index), index, 2, row_peer)),
                    (exists, full_copy(held(index), index, 3, core_peer)),
                ]
                relays.append((hop, exists, index, made))
    crossed = []
    for step in range(layers):
        for base in (row_peer, depth * 4 + (1 - row) * 2 + (1 - core)):
            index = (base + 4 * step) % count
            crossed.append((index, full_copy(held(index), index, 3, core_peer)))

    own_copy = remote(
        weight_hbm, held(me), full_send.at[3], full_recv.at[me], {"hs": core_peer}
    )

    @pl.when(owner)
    def _():
        own_copy.start()

    @pl.when(helper)
    def _():
        for copy in outgoing:
            copy.start()
        start_all(first_sends)

    for i in range(max(2, layers - 2)):
        greet(ready.at[i])
        pl.semaphore_wait(ready.at[i], link_count)

    @pl.when(helper)
    def _():
        arrived(core_peer)
        start_all(second_sends)

    side_copy.wait()
    spread = side[...].astype(jnp.float32)
    for seq in range(seq_count):
        moved[seq] = spread[:, seq, :].astype(jnp.bfloat16)
    gate_copies = [
        remote(
            moved.at[order[step]],
            gates.at[depth],
            gate_send,
            gate_recv.at[depth],
            {"hs": order[step] * 4 + inner},
        )
        for step in range(last)
    ]

    @pl.when(helper)
    def _():
        opened_hop = max(1, layers - 2)
        for position, (hop, exists, index, made) in enumerate(relays):
            pl.when(exists)(functools.partial(arrived, index))
            start_all(made)
            if hop == opened_hop and position + 1 == 4 * opened_hop:
                for copy in gate_copies:
                    copy.start()
        for index, copy in crossed:
            arrived(index)
            copy.start()

    def learn(start, rate, first):
        key_part = keys[rows(start, piece), :]
        rate_column = jnp.broadcast_to(rate, (128, piece)).T[:, :1]
        scaled_part = (rate_column * values[rows(start, piece), :].astype(jnp.float32)).astype(
            jnp.bfloat16
        )
        pre_gate = inner_cols(key_part, fast[0])
        pre_up = inner_cols(key_part, fast[1])
        sig_gate = jax.nn.sigmoid(pre_gate)
        act_gate = pre_gate * sig_gate
        hidden = (act_gate * pre_up).astype(jnp.bfloat16)
        back_hidden = jnp.dot(scaled_part, fast[2], preferred_element_type=jnp.float32)
        back_gate = (
            back_hidden * pre_up * sig_gate * (1.0 + pre_gate * (1.0 - sig_gate))
        ).astype(jnp.bfloat16)
        back_up = (back_hidden * act_gate).astype(jnp.bfloat16)
        terms = (
            inner_rows(back_gate, key_part),
            inner_rows(back_up, key_part),
            inner_rows(scaled_part, hidden),
        )
        for i, term in enumerate(terms):
            grads[i] = term if first else grads[i] + term

    head_copies = {}
    for half in (other, ctx):
        for step in range(layers):
            start = half * tokens + order[step] * step_rows
            for i in range(3 if half is ctx else 4):
                place = (inner + 1 + i) % 4
                head_copies[half is ctx, step, i] = remote(
                    heads.at[rows(start + place * block_rows, block_rows)],
                    mixed.at[order[step], row * 2 + ctx],
                    head_send,
                    head_recv.at[order[step]],
                    {"ctx": half, "hs": depth * 4 + place},
                )

    def answer(half, step):
        target = order[step]
        start = half * tokens + target * step_rows
        query_part = queries[rows(start, step_rows), :]
        query_gate = inner_cols(query_part, fresh[0])
        query_up = inner_cols(query_part, fresh[1])
        query_hidden = (query_gate * jax.nn.sigmoid(query_gate) * query_up).astype(jnp.bfloat16)
        heads[rows(start, step_rows), :] = inner_cols(query_hidden, fresh[2]).astype(jnp.bfloat16)
        for i in range(4):
            if half is ctx and i == 3:
                mixed[target, row * 2 + ctx] = heads[
                    rows(start + inner * block_rows, block_rows), :
                ]
            else:
                head_copies[half is ctx, step, i].start()

    @pl.when(owner)
    def _():
        drain(lines(3 * part + 3 * tokens), local_sem.at[0])
        own_rates.wait()
        drain(lines(3 * part), ctx_recv.at[1])
        for j in range(pieces):
            learn(ctx * tokens + j * piece, rates[ctx, :, j * piece : (j + 1) * piece], j == 0)
        drain(rates.at[other], ctx_recv.at[0])
        for j in range(pieces):
            drain(lines(2 * piece), ctx_recv.at[2 + j])
            if j == 0:
                for copy in gate_copies:
                    copy.start()
            learn(
                other * tokens + j * piece, rates[other, :, j * piece : (j + 1) * piece], False
            )
        for i in range(3):
            fresh[i] = rescale_rows(fast[i], grads[i])
        for step in range(layers):
            drain(lines(step_rows), ctx_recv.at[2 + pieces + step])
            answer(other, step)
            answer(ctx, step)
        for step in range(1, count):
            arrived((me + step) % count)

    own_shard.wait()
    gain_copy.wait()
    for step in range(layers):
        target = order[step]

        @pl.when(owner)
        def _():
            drain(mixed.at[target, pl.ds(0, 3)], head_recv.at[target])

        @pl.when(helper)
        def _():
            drain(mixed.at[target], head_recv.at[target])

        if step < last:
            drain(gates.at[target], gate_recv.at[target])
            opened = gates[target]
        else:
            opened = moved[depth]
        opened = opened.astype(jnp.float32)
        opened = opened * jax.nn.sigmoid(opened)
        for head in range(head_count):
            columns = slice(head * size, (head + 1) * size)
            value = mixed[target, head].astype(jnp.float32)
            square = jnp.mean(value * value, -1, keepdims=True)
            value = value * lax.rsqrt(square + epsilon) * gain[:, columns]
            normed[step, :, columns] = (value * opened[:, columns]).astype(jnp.bfloat16)
        result = jnp.dot(normed[step], full[...], preferred_element_type=jnp.float32)
        outs[step] = result.astype(jnp.bfloat16)
        if step < last:
            copy = remote(
                outs.at[step],
                out_ref.at[depth],
                out_send,
                out_recv,
                {"hs": target * 4 + inner},
            )
        else:
            copy = pltpu.make_async_copy(outs.at[step], out_ref.at[depth], local_sem.at[2])
        copy.start()

    @pl.when(owner)
    def _():
        drain(held(0), full_send.at[3])
        drain(heads.at[pl.ds(0, 7 * layers * block_rows)], head_send)

    def sent(amount, way):
        if amount:
            drain(full.at[pl.ds(0, amount * shard)], full_send.at[way])

    @pl.when(helper)
    def _():
        drain(rates.at[ctx], ctx_send.at[0])
        drain(lines(3 * part + 3 * tokens), ctx_send.at[1])
        for layer in range(layers):

            @pl.when(depth == layer)
            def _():
                sent(2 + 2 * layer if layer < last else 0, 0)
                sent(2 + 2 * (last - layer) if layer > 0 else 0, 1)

        sent(2 * layers, 2)
        sent(4 * layers - 1, 3)

    drain(moved.at[pl.ds(0, last)], gate_send)
    drain(outs.at[pl.ds(0, last)], out_send)
    drain(outs.at[pl.ds(0, last)], out_recv)
    drain(outs.at[0], local_sem.at[2])


def swapped_body(
    key_rows,
    value_rows,
    query_rows,
    step_rates,
    fast_gate,
    fast_up,
    fast_down,
    out_gain,
    gate_input,
    out_weight,
):
    layers = lax.axis_size("hs") // 4
    count = 4 * layers
    pieces = 2
    tokens, size = key_rows.shape[1:]
    hidden_size = 2 * fast_gate.shape[1]
    block_rows, seq_count, width = gate_input.shape
    columns = out_weight.shape[1]
    anywhere = pl.BlockSpec(memory_space=pl.ANY)
    half = jnp.bfloat16
    dma = pltpu.SemaphoreType.DMA
    laid = pl.pallas_call(
        functools.partial(layer_kernel, layers, pieces),
        out_shape=jax.ShapeDtypeStruct((seq_count, block_rows, columns), half),
        in_specs=[anywhere] * 10,
        out_specs=anywhere,
        scratch_shapes=[
            pltpu.VMEM((3, hidden_size, size), half),
            pltpu.VMEM((3, hidden_size, size), half),
            pltpu.VMEM((2 * tokens, size), half),
            pltpu.VMEM((2 * tokens, size), half),
            pltpu.VMEM((2, 1, tokens), jnp.float32),
            pltpu.VMEM((2 * tokens, size), half),
            pltpu.VMEM((1, width), jnp.float32),
            pltpu.VMEM((block_rows, seq_count, width), half),
            pltpu.VMEM((seq_count, block_rows, width), half),
            pltpu.VMEM((layers, block_rows, width), half),
            pltpu.VMEM((width, columns), half),
            pltpu.VMEM((3, hidden_size, size), jnp.float32),
            pltpu.VMEM((2 * tokens, size), half),
            pltpu.VMEM((layers, 4, block_rows, size), half),
            pltpu.VMEM((layers, block_rows, width), half),
            pltpu.VMEM((layers, block_rows, columns), half),
            dma((5,)),
            dma((2,)),
            dma((2 + pieces + layers,)),
            dma((4,)),
            dma((count,)),
            dma(()),
            dma((layers,)),
            dma(()),
            dma((layers,)),
            dma(()),
            dma(()),
            pltpu.SemaphoreType.REGULAR((max(2, layers - 2),)),
        ],
        compiler_params=pltpu.CompilerParams(
            collective_id=0, has_side_effects=True, vmem_limit_bytes=60 * 1024 * 1024
        ),
    )(
        fast_gate,
        fast_up,
        fast_down,
        key_rows,
        value_rows,
        query_rows,
        gate_input,
        out_weight,
        step_rates,
        out_gain[None],
    )
    return laid.transpose(1, 0, 2)


def solution(mesh):
    def step(*arrays):
        paired = mesh.shape["ctx"] == 2 and mesh.shape["hs"] % 8 == 0
        paired = paired and arrays[0].shape[0] == 1
        paired = paired and arrays[8].shape[1] == mesh.shape["hs"] // 4
        paired = paired and arrays[8].shape[2] == 4 * arrays[0].shape[2]
        return (swapped_body if paired else body)(*arrays)

    return jax.shard_map(
        step,
        mesh=mesh,
        in_specs=(
            P("hs", "ctx", None),
            P("hs", "ctx", None),
            P("hs", "ctx", None),
            P("hs", "ctx"),
            P("hs", "ctx", None),
            P("hs", "ctx", None),
            P("hs", "ctx", None),
            P(),
            P(("ctx", "hs"), None, None),
            P("hs", None),
        ),
        out_specs=P(("ctx", "hs"), None, None),
        check_vma=False,
    )
```

```python
import functools

import jax
import jax.numpy as jnp
from jax import lax
from jax.experimental import pallas as pl
from jax.experimental.pallas import tpu as pltpu
from jax.sharding import PartitionSpec as P

epsilon = 1e-06


def rescale_rows(weight, update):
    base = weight.astype(jnp.float32)
    moved = base + update
    factor = jnp.sqrt(jnp.mean(base * base, -1, keepdims=True) + epsilon) / jnp.sqrt(
        jnp.mean(moved * moved, -1, keepdims=True) + epsilon
    )
    return (moved * factor).astype(jnp.bfloat16)


def inner_rows(left, right):
    return lax.dot_general(
        left, right, (((0,), (0,)), ((), ())), preferred_element_type=jnp.float32
    )


def body(
    key_rows,
    value_rows,
    query_rows,
    step_rates,
    fast_gate,
    fast_up,
    fast_down,
    out_gain,
    gate_input,
    out_weight,
):
    key_row = key_rows[0]
    value_row = value_rows[0]
    query_row = query_rows[0]
    rate_row = step_rates[0]
    whole_gate, whole_up, whole_down = (
        lax.all_gather(fast_gate, "ctx", axis=1, tiled=True),
        lax.all_gather(fast_up, "ctx", axis=1, tiled=True),
        lax.all_gather(fast_down, "ctx", axis=1, tiled=True),
    )
    gate_fast = whole_gate[0]
    up_fast = whole_up[0]
    down_fast = whole_down[0]
    pre_gate = jnp.dot(key_row, gate_fast.T, preferred_element_type=jnp.float32)
    pre_up = jnp.dot(key_row, up_fast.T, preferred_element_type=jnp.float32)
    sig_gate = jax.nn.sigmoid(pre_gate)
    act_gate = pre_gate * sig_gate
    hidden = (act_gate * pre_up).astype(jnp.bfloat16)
    scaled = (rate_row[:, None] * value_row.astype(jnp.float32)).astype(jnp.bfloat16)
    grad_down = inner_rows(scaled, hidden)
    back_hidden = jnp.dot(scaled, down_fast, preferred_element_type=jnp.float32)
    back_gate = (back_hidden * pre_up * sig_gate * (1.0 + pre_gate * (1.0 - sig_gate))).astype(
        jnp.bfloat16
    )
    back_up = (back_hidden * act_gate).astype(jnp.bfloat16)
    grad_gate = inner_rows(back_gate, key_row)
    grad_up = inner_rows(back_up, key_row)
    grad_gate, grad_up, grad_down = (
        lax.psum_scatter(grad_gate, "ctx", scatter_dimension=0, tiled=True),
        lax.psum_scatter(grad_up, "ctx", scatter_dimension=0, tiled=True),
        lax.psum_scatter(grad_down, "ctx", scatter_dimension=0, tiled=True),
    )
    part_gate = rescale_rows(fast_gate[0], grad_gate)
    part_up = rescale_rows(fast_up[0], grad_up)
    part_down = rescale_rows(fast_down[0], grad_down)
    new_gate, new_up, new_down = (
        lax.all_gather(part_gate, "ctx", axis=0, tiled=True),
        lax.all_gather(part_up, "ctx", axis=0, tiled=True),
        lax.all_gather(part_down, "ctx", axis=0, tiled=True),
    )
    query_gate = jnp.dot(query_row, new_gate.T, preferred_element_type=jnp.float32)
    query_up = jnp.dot(query_row, new_up.T, preferred_element_type=jnp.float32)
    query_hidden = (jax.nn.silu(query_gate) * query_up).astype(jnp.bfloat16)
    head_out = jnp.dot(query_hidden, new_down.T, preferred_element_type=jnp.float32).astype(
        jnp.bfloat16
    )
    width_hs = lax.axis_size("hs")
    head_size = head_out.shape[1]
    token_count = head_out.shape[0] // width_hs
    blocks = head_out.reshape(width_hs, token_count, head_size)
    moved = lax.all_to_all(blocks, "hs", split_axis=0, concat_axis=2, tiled=True)
    seq_count = gate_input.shape[1]
    model_width = gate_input.shape[2]
    head_count = model_width // head_size
    mixed = moved.reshape(token_count, seq_count, head_count, head_size).astype(jnp.float32)
    square = jnp.mean(mixed * mixed, -1, keepdims=True)
    scaled_heads = mixed * lax.rsqrt(square + epsilon) * out_gain.reshape(head_count, head_size)
    normed = (
        scaled_heads.reshape(token_count, seq_count, model_width)
        * jax.nn.silu(gate_input.astype(jnp.float32))
    ).astype(jnp.bfloat16)
    flat_rows = normed.reshape(token_count * seq_count, model_width)
    out_cols = out_weight.shape[1]
    full_weight = lax.all_gather(out_weight, "hs", axis=0, tiled=True)
    result = jnp.dot(flat_rows, full_weight, preferred_element_type=jnp.float32)
    return result.astype(jnp.bfloat16).reshape(token_count, seq_count, out_cols)


MESH = pl.DeviceIdType.MESH


def inner_cols(left, right):
    return lax.dot_general(
        left, right, (((1,), (1,)), ((), ())), preferred_element_type=jnp.float32
    )


def layer_kernel(
    layers,
    pieces,
    gate_hbm,
    up_hbm,
    down_hbm,
    key_hbm,
    value_hbm,
    query_hbm,
    side_hbm,
    weight_hbm,
    rate_hbm,
    gain_hbm,
    out_ref,
    fast,
    fresh,
    keys,
    values,
    rates,
    queries,
    gain,
    side,
    moved,
    gates,
    full,
    grads,
    heads,
    mixed,
    normed,
    outs,
    local_sem,
    ctx_send,
    ctx_recv,
    full_send,
    full_recv,
    gate_send,
    gate_recv,
    head_send,
    head_recv,
    out_send,
    out_recv,
    ready,
):
    ctx = lax.axis_index("ctx")
    me = lax.axis_index("hs")
    other = 1 - ctx
    count = 4 * layers
    last = layers - 1
    depth, inner = me // 4, me % 4
    row, core = inner // 2, inner % 2
    row_peer = depth * 4 + (1 - row) * 2 + core
    core_peer = depth * 4 + row * 2 + (1 - core)
    owner = core == ctx
    helper = core != ctx
    part = gate_hbm.shape[1]
    tokens = key_hbm.shape[1]
    piece = tokens // pieces
    shard = weight_hbm.shape[0]
    block_rows = tokens // count
    step_rows = 4 * block_rows
    seq_count = side.shape[1]
    size = key_hbm.shape[2]
    head_count = side.shape[2] // size

    def remote(source, target, send, recv, device):
        return pltpu.make_async_remote_copy(
            src_ref=source,
            dst_ref=target,
            send_sem=send,
            recv_sem=recv,
            device_id=device,
            device_id_type=MESH,
        )

    def rows(start, size):
        return pl.ds(pl.multiple_of(start, size), size)

    def drain(block, semaphore):
        pltpu.make_async_copy(block, block, semaphore).wait()

    def guarded(condition, action):
        if condition is None:
            action()
        else:
            pl.when(condition)(action)

    links = [
        (None, {"ctx": other}),
        (None, {"hs": row_peer}),
        (None, {"hs": core_peer}),
        (depth < last, {"hs": me + 4}),
        (depth > 0, {"hs": me - 4}),
    ]
    link_count = 3 + jnp.where(depth < last, 1, 0) + jnp.where(depth > 0, 1, 0)

    def greet(semaphore):
        for condition, device in links:
            guarded(
                condition,
                functools.partial(
                    pl.semaphore_signal, semaphore, inc=1, device_id=device, device_id_type=MESH
                ),
            )

    barrier = pltpu.get_barrier_semaphore()
    greet(barrier)

    weights = (gate_hbm, up_hbm, down_hbm)
    near = rows(ctx * tokens, tokens)
    owned = [
        pltpu.make_async_copy(source, target, local_sem.at[0])
        for source, target in [
            (source.at[0], fast.at[i, rows(ctx * part, part)])
            for i, source in enumerate(weights)
        ]
        + [
            (source.at[0], target.at[near])
            for source, target in ((key_hbm, keys), (value_hbm, values), (query_hbm, queries))
        ]
    ]
    own_rates = pltpu.make_async_copy(rate_hbm, rates.at[ctx], local_sem.at[1])
    side_copy = pltpu.make_async_copy(side_hbm, side, local_sem.at[2])
    own_shard = pltpu.make_async_copy(
        weight_hbm, full.at[rows(me * shard, shard)], local_sem.at[3]
    )
    gain_copy = pltpu.make_async_copy(gain_hbm, gain, local_sem.at[4])

    @pl.when(owner)
    def _():
        for copy in owned:
            copy.start()
        own_rates.start()

    for copy in (side_copy, own_shard, gain_copy):
        copy.start()
    pl.semaphore_wait(barrier, link_count)

    mid = layers // 2
    side_half = (depth // mid) * mid
    order = [mid - side_half + (depth + step) % mid for step in range(mid)]
    order += [side_half + (depth + step) % mid for step in range(1, mid)] + [depth]

    swaps = [(rate_hbm, lambda who: rates.at[who])]
    for i, source in enumerate(weights):
        swaps.append((source.at[0], lambda who, i=i: fast.at[i, rows(who * part, part)]))
    for j in range(pieces):
        for source, target in ((key_hbm.at[0], keys), (value_hbm.at[0], values)):
            swaps.append(
                (
                    source.at[pl.ds(j * piece, piece)],
                    lambda who, target=target, j=j: target.at[
                        rows(who * tokens + j * piece, piece)
                    ],
                )
            )
    for step in range(layers):
        swaps.append(
            (
                query_hbm.at[0, rows(order[step] * step_rows, step_rows)],
                lambda who, step=step: queries.at[
                    rows(who * tokens + order[step] * step_rows, step_rows)
                ],
            )
        )
    arrivals = [0, 1, 1, 1]
    arrivals += [2 + j for j in range(pieces) for _ in range(2)]
    arrivals += [2 + pieces + step for step in range(layers)]
    outgoing = [
        remote(
            source,
            target(ctx),
            ctx_send.at[0 if i == 0 else 1],
            ctx_recv.at[arrivals[i]],
            {"ctx": other},
        )
        for i, (source, target) in enumerate(swaps)
    ]
    def lines(count):
        return full.at[pl.ds(0, count * size // full.shape[1])]

    def held(index):
        return full.at[rows(index * shard, shard)]

    def full_copy(source, index, way, device):
        return remote(source, held(index), full_send.at[way], full_recv.at[index], {"hs": device})

    def arrived(index):
        block = held(index)
        remote(block, block, full_send.at[0], full_recv.at[index], {"hs": core_peer}).wait_recv()

    def start_all(made):
        for condition, copy in made:
            guarded(condition, copy.start)

    first_sends = [
        (None, full_copy(weight_hbm, me, 3, core_peer)),
        (depth < last, full_copy(weight_hbm, me, 0, me + 4)),
        (depth > 0, full_copy(weight_hbm, me, 1, me - 4)),
        (None, full_copy(weight_hbm, me, 2, row_peer)),
    ]
    second_sends = [
        (depth < last, full_copy(held(core_peer), core_peer, 0, me + 4)),
        (depth > 0, full_copy(held(core_peer), core_peer, 1, me - 4)),
        (None, full_copy(held(core_peer), core_peer, 2, row_peer)),
    ]
    relays = []
    for hop in range(1, layers):
        for base in (me, core_peer):
            for upward in (True, False):
                exists = depth >= hop if upward else depth + hop <= last
                onward = depth < last if upward else depth > 0
                index = base - 4 * hop if upward else base + 4 * hop
                next_device = me + 4 if upward else me - 4
                made = [
                    (exists & onward, full_copy(held(index), index, 0 if upward else 1, next_device)),
                    (exists, full_copy(held(index), index, 2, row_peer)),
                    (exists, full_copy(held(index), index, 3, core_peer)),
                ]
                relays.append((hop, exists, index, made))
    crossed = []
    for step in range(layers):
        for base in (row_peer, depth * 4 + (1 - row) * 2 + (1 - core)):
            index = (base + 4 * step) % count
            crossed.append((index, full_copy(held(index), index, 3, core_peer)))

    own_copy = remote(
        weight_hbm, held(me), full_send.at[3], full_recv.at[me], {"hs": core_peer}
    )

    @pl.when(owner)
    def _():
        own_copy.start()

    @pl.when(helper)
    def _():
        for copy in outgoing:
            copy.start()
        start_all(first_sends)

    for i in range(max(2, layers - 2)):
        greet(ready.at[i])
        pl.semaphore_wait(ready.at[i], link_count)

    @pl.when(helper)
    def _():
        arrived(core_peer)
        start_all(second_sends)

    side_copy.wait()
    spread = side[...].astype(jnp.float32)
    for seq in range(seq_count):
        moved[seq] = spread[:, seq, :].astype(jnp.bfloat16)
    gate_copies = [
        remote(
            moved.at[order[step]],
            gates.at[depth],
            gate_send,
            gate_recv.at[depth],
            {"hs": order[step] * 4 + inner},
        )
        for step in range(last)
    ]

    @pl.when(helper)
    def _():
        for position, (hop, exists, index, made) in enumerate(relays):
            pl.when(exists)(functools.partial(arrived, index))
            start_all(made)
        for turn, (index, copy) in enumerate(crossed):
            if turn == layers:
                for gate_copy in gate_copies:
                    gate_copy.start()
            arrived(index)
            copy.start()

    def learn(start, rate, first):
        key_part = keys[rows(start, piece), :]
        rate_column = jnp.broadcast_to(rate, (128, piece)).T[:, :1]
        scaled_part = (rate_column * values[rows(start, piece), :].astype(jnp.float32)).astype(
            jnp.bfloat16
        )
        pre_gate = inner_cols(key_part, fast[0])
        pre_up = inner_cols(key_part, fast[1])
        sig_gate = jax.nn.sigmoid(pre_gate)
        act_gate = pre_gate * sig_gate
        hidden = (act_gate * pre_up).astype(jnp.bfloat16)
        back_hidden = jnp.dot(scaled_part, fast[2], preferred_element_type=jnp.float32)
        back_gate = (
            back_hidden * pre_up * sig_gate * (1.0 + pre_gate * (1.0 - sig_gate))
        ).astype(jnp.bfloat16)
        back_up = (back_hidden * act_gate).astype(jnp.bfloat16)
        terms = (
            inner_rows(back_gate, key_part),
            inner_rows(back_up, key_part),
            inner_rows(scaled_part, hidden),
        )
        for i, term in enumerate(terms):
            grads[i] = term if first else grads[i] + term

    head_copies = {}
    for half in (other, ctx):
        for step in range(layers):
            start = half * tokens + order[step] * step_rows
            for i in range(3 if half is ctx else 4):
                place = (inner + 1 + i) % 4
                head_copies[half is ctx, step, i] = remote(
                    heads.at[rows(start + place * block_rows, block_rows)],
                    mixed.at[order[step], row * 2 + ctx],
                    head_send,
                    head_recv.at[order[step]],
                    {"ctx": half, "hs": depth * 4 + place},
                )

    def answer(half, step):
        target = order[step]
        start = half * tokens + target * step_rows
        query_part = queries[rows(start, step_rows), :]
        query_gate = inner_cols(query_part, fresh[0])
        query_up = inner_cols(query_part, fresh[1])
        query_hidden = (query_gate * jax.nn.sigmoid(query_gate) * query_up).astype(jnp.bfloat16)
        heads[rows(start, step_rows), :] = inner_cols(query_hidden, fresh[2]).astype(jnp.bfloat16)
        for i in range(4):
            if half is ctx and i == 3:
                mixed[target, row * 2 + ctx] = heads[
                    rows(start + inner * block_rows, block_rows), :
                ]
            else:
                head_copies[half is ctx, step, i].start()

    @pl.when(owner)
    def _():
        drain(lines(3 * part + 3 * tokens), local_sem.at[0])
        own_rates.wait()
        drain(lines(3 * part), ctx_recv.at[1])
        for j in range(pieces):
            learn(ctx * tokens + j * piece, rates[ctx, :, j * piece : (j + 1) * piece], j == 0)
        drain(rates.at[other], ctx_recv.at[0])
        for j in range(pieces):
            drain(lines(2 * piece), ctx_recv.at[2 + j])
            if j == pieces - 1:
                for copy in gate_copies:
                    copy.start()
            learn(
                other * tokens + j * piece, rates[other, :, j * piece : (j + 1) * piece], False
            )
        for i in range(3):
            fresh[i] = rescale_rows(fast[i], grads[i])
        for step in range(layers):
            drain(lines(step_rows), ctx_recv.at[2 + pieces + step])
            answer(other, step)
            answer(ctx, step)
        for step in range(1, count):
            arrived((me + step) % count)

    own_shard.wait()
    gain_copy.wait()
    for step in range(layers):
        target = order[step]

        @pl.when(owner)
        def _():
            drain(mixed.at[target, pl.ds(0, 3)], head_recv.at[target])

        @pl.when(helper)
        def _():
            drain(mixed.at[target], head_recv.at[target])

        if step < last:
            drain(gates.at[target], gate_recv.at[target])
            opened = gates[target]
        else:
            opened = moved[depth]
        opened = opened.astype(jnp.float32)
        opened = opened * jax.nn.sigmoid(opened)
        for head in range(head_count):
            columns = slice(head * size, (head + 1) * size)
            value = mixed[target, head].astype(jnp.float32)
            square = jnp.mean(value * value, -1, keepdims=True)
            value = value * lax.rsqrt(square + epsilon) * gain[:, columns]
            normed[step, :, columns] = (value * opened[:, columns]).astype(jnp.bfloat16)
        result = jnp.dot(normed[step], full[...], preferred_element_type=jnp.float32)
        outs[step] = result.astype(jnp.bfloat16)
        if step < last:
            copy = remote(
                outs.at[step],
                out_ref.at[depth],
                out_send,
                out_recv,
                {"hs": target * 4 + inner},
            )
        else:
            copy = pltpu.make_async_copy(outs.at[step], out_ref.at[depth], local_sem.at[2])
        copy.start()

    @pl.when(owner)
    def _():
        drain(held(0), full_send.at[3])
        drain(heads.at[pl.ds(0, 7 * layers * block_rows)], head_send)

    def sent(amount, way):
        if amount:
            drain(full.at[pl.ds(0, amount * shard)], full_send.at[way])

    @pl.when(helper)
    def _():
        drain(rates.at[ctx], ctx_send.at[0])
        drain(lines(3 * part + 3 * tokens), ctx_send.at[1])
        for layer in range(layers):

            @pl.when(depth == layer)
            def _():
                sent(2 + 2 * layer if layer < last else 0, 0)
                sent(2 + 2 * (last - layer) if layer > 0 else 0, 1)

        sent(2 * layers, 2)
        sent(4 * layers - 1, 3)

    drain(moved.at[pl.ds(0, last)], gate_send)
    drain(outs.at[pl.ds(0, last)], out_send)
    drain(outs.at[pl.ds(0, last)], out_recv)
    drain(outs.at[0], local_sem.at[2])


def swapped_body(
    key_rows,
    value_rows,
    query_rows,
    step_rates,
    fast_gate,
    fast_up,
    fast_down,
    out_gain,
    gate_input,
    out_weight,
):
    layers = lax.axis_size("hs") // 4
    count = 4 * layers
    pieces = 2
    tokens, size = key_rows.shape[1:]
    hidden_size = 2 * fast_gate.shape[1]
    block_rows, seq_count, width = gate_input.shape
    columns = out_weight.shape[1]
    anywhere = pl.BlockSpec(memory_space=pl.ANY)
    half = jnp.bfloat16
    dma = pltpu.SemaphoreType.DMA
    laid = pl.pallas_call(
        functools.partial(layer_kernel, layers, pieces),
        out_shape=jax.ShapeDtypeStruct((seq_count, block_rows, columns), half),
        in_specs=[anywhere] * 10,
        out_specs=anywhere,
        scratch_shapes=[
            pltpu.VMEM((3, hidden_size, size), half),
            pltpu.VMEM((3, hidden_size, size), half),
            pltpu.VMEM((2 * tokens, size), half),
            pltpu.VMEM((2 * tokens, size), half),
            pltpu.VMEM((2, 1, tokens), jnp.float32),
            pltpu.VMEM((2 * tokens, size), half),
            pltpu.VMEM((1, width), jnp.float32),
            pltpu.VMEM((block_rows, seq_count, width), half),
            pltpu.VMEM((seq_count, block_rows, width), half),
            pltpu.VMEM((layers, block_rows, width), half),
            pltpu.VMEM((width, columns), half),
            pltpu.VMEM((3, hidden_size, size), jnp.float32),
            pltpu.VMEM((2 * tokens, size), half),
            pltpu.VMEM((layers, 4, block_rows, size), half),
            pltpu.VMEM((layers, block_rows, width), half),
            pltpu.VMEM((layers, block_rows, columns), half),
            dma((5,)),
            dma((2,)),
            dma((2 + pieces + layers,)),
            dma((4,)),
            dma((count,)),
            dma(()),
            dma((layers,)),
            dma(()),
            dma((layers,)),
            dma(()),
            dma(()),
            pltpu.SemaphoreType.REGULAR((max(2, layers - 2),)),
        ],
        compiler_params=pltpu.CompilerParams(
            collective_id=0, has_side_effects=True, vmem_limit_bytes=60 * 1024 * 1024
        ),
    )(
        fast_gate,
        fast_up,
        fast_down,
        key_rows,
        value_rows,
        query_rows,
        gate_input,
        out_weight,
        step_rates,
        out_gain[None],
    )
    return laid.transpose(1, 0, 2)


def solution(mesh):
    def step(*arrays):
        paired = mesh.shape["ctx"] == 2 and mesh.shape["hs"] % 8 == 0
        paired = paired and arrays[0].shape[0] == 1
        paired = paired and arrays[8].shape[1] == mesh.shape["hs"] // 4
        paired = paired and arrays[8].shape[2] == 4 * arrays[0].shape[2]
        return (swapped_body if paired else body)(*arrays)

    return jax.shard_map(
        step,
        mesh=mesh,
        in_specs=(
            P("hs", "ctx", None),
            P("hs", "ctx", None),
            P("hs", "ctx", None),
            P("hs", "ctx"),
            P("hs", "ctx", None),
            P("hs", "ctx", None),
            P("hs", "ctx", None),
            P(),
            P(("ctx", "hs"), None, None),
            P("hs", None),
        ),
        out_specs=P(("ctx", "hs"), None, None),
        check_vma=False,
    )
```

```python
import functools

import jax
import jax.numpy as jnp
from jax import lax
from jax.experimental import pallas as pl
from jax.experimental.pallas import tpu as pltpu
from jax.sharding import PartitionSpec as P

epsilon = 1e-06


def rescale_rows(weight, update):
    base = weight.astype(jnp.float32)
    moved = base + update
    factor = jnp.sqrt(jnp.mean(base * base, -1, keepdims=True) + epsilon) / jnp.sqrt(
        jnp.mean(moved * moved, -1, keepdims=True) + epsilon
    )
    return (moved * factor).astype(jnp.bfloat16)


def inner_rows(left, right):
    return lax.dot_general(
        left, right, (((0,), (0,)), ((), ())), preferred_element_type=jnp.float32
    )


def body(
    key_rows,
    value_rows,
    query_rows,
    step_rates,
    fast_gate,
    fast_up,
    fast_down,
    out_gain,
    gate_input,
    out_weight,
):
    key_row = key_rows[0]
    value_row = value_rows[0]
    query_row = query_rows[0]
    rate_row = step_rates[0]
    whole_gate, whole_up, whole_down = (
        lax.all_gather(fast_gate, "ctx", axis=1, tiled=True),
        lax.all_gather(fast_up, "ctx", axis=1, tiled=True),
        lax.all_gather(fast_down, "ctx", axis=1, tiled=True),
    )
    gate_fast = whole_gate[0]
    up_fast = whole_up[0]
    down_fast = whole_down[0]
    pre_gate = jnp.dot(key_row, gate_fast.T, preferred_element_type=jnp.float32)
    pre_up = jnp.dot(key_row, up_fast.T, preferred_element_type=jnp.float32)
    sig_gate = jax.nn.sigmoid(pre_gate)
    act_gate = pre_gate * sig_gate
    hidden = (act_gate * pre_up).astype(jnp.bfloat16)
    scaled = (rate_row[:, None] * value_row.astype(jnp.float32)).astype(jnp.bfloat16)
    grad_down = inner_rows(scaled, hidden)
    back_hidden = jnp.dot(scaled, down_fast, preferred_element_type=jnp.float32)
    back_gate = (back_hidden * pre_up * sig_gate * (1.0 + pre_gate * (1.0 - sig_gate))).astype(
        jnp.bfloat16
    )
    back_up = (back_hidden * act_gate).astype(jnp.bfloat16)
    grad_gate = inner_rows(back_gate, key_row)
    grad_up = inner_rows(back_up, key_row)
    grad_gate, grad_up, grad_down = (
        lax.psum_scatter(grad_gate, "ctx", scatter_dimension=0, tiled=True),
        lax.psum_scatter(grad_up, "ctx", scatter_dimension=0, tiled=True),
        lax.psum_scatter(grad_down, "ctx", scatter_dimension=0, tiled=True),
    )
    part_gate = rescale_rows(fast_gate[0], grad_gate)
    part_up = rescale_rows(fast_up[0], grad_up)
    part_down = rescale_rows(fast_down[0], grad_down)
    new_gate, new_up, new_down = (
        lax.all_gather(part_gate, "ctx", axis=0, tiled=True),
        lax.all_gather(part_up, "ctx", axis=0, tiled=True),
        lax.all_gather(part_down, "ctx", axis=0, tiled=True),
    )
    query_gate = jnp.dot(query_row, new_gate.T, preferred_element_type=jnp.float32)
    query_up = jnp.dot(query_row, new_up.T, preferred_element_type=jnp.float32)
    query_hidden = (jax.nn.silu(query_gate) * query_up).astype(jnp.bfloat16)
    head_out = jnp.dot(query_hidden, new_down.T, preferred_element_type=jnp.float32).astype(
        jnp.bfloat16
    )
    width_hs = lax.axis_size("hs")
    head_size = head_out.shape[1]
    token_count = head_out.shape[0] // width_hs
    blocks = head_out.reshape(width_hs, token_count, head_size)
    moved = lax.all_to_all(blocks, "hs", split_axis=0, concat_axis=2, tiled=True)
    seq_count = gate_input.shape[1]
    model_width = gate_input.shape[2]
    head_count = model_width // head_size
    mixed = moved.reshape(token_count, seq_count, head_count, head_size).astype(jnp.float32)
    square = jnp.mean(mixed * mixed, -1, keepdims=True)
    scaled_heads = mixed * lax.rsqrt(square + epsilon) * out_gain.reshape(head_count, head_size)
    normed = (
        scaled_heads.reshape(token_count, seq_count, model_width)
        * jax.nn.silu(gate_input.astype(jnp.float32))
    ).astype(jnp.bfloat16)
    flat_rows = normed.reshape(token_count * seq_count, model_width)
    out_cols = out_weight.shape[1]
    full_weight = lax.all_gather(out_weight, "hs", axis=0, tiled=True)
    result = jnp.dot(flat_rows, full_weight, preferred_element_type=jnp.float32)
    return result.astype(jnp.bfloat16).reshape(token_count, seq_count, out_cols)


MESH = pl.DeviceIdType.MESH


def inner_cols(left, right):
    return lax.dot_general(
        left, right, (((1,), (1,)), ((), ())), preferred_element_type=jnp.float32
    )


def layer_kernel(
    layers,
    pieces,
    gate_hbm,
    up_hbm,
    down_hbm,
    key_hbm,
    value_hbm,
    query_hbm,
    side_hbm,
    weight_hbm,
    rate_hbm,
    gain_hbm,
    out_ref,
    fast,
    fresh,
    keys,
    values,
    rates,
    queries,
    gain,
    side,
    moved,
    gates,
    full,
    grads,
    heads,
    mixed,
    normed,
    outs,
    local_sem,
    ctx_send,
    ctx_recv,
    full_send,
    full_recv,
    gate_send,
    gate_recv,
    head_send,
    head_recv,
    out_send,
    out_recv,
    ready,
):
    ctx = lax.axis_index("ctx")
    me = lax.axis_index("hs")
    other = 1 - ctx
    count = 4 * layers
    last = layers - 1
    depth, inner = me // 4, me % 4
    row, core = inner // 2, inner % 2
    row_peer = depth * 4 + (1 - row) * 2 + core
    core_peer = depth * 4 + row * 2 + (1 - core)
    owner = core == ctx
    helper = core != ctx
    part = gate_hbm.shape[1]
    tokens = key_hbm.shape[1]
    piece = tokens // pieces
    shard = weight_hbm.shape[0]
    block_rows = tokens // count
    step_rows = 4 * block_rows
    seq_count = side.shape[1]
    size = key_hbm.shape[2]
    head_count = side.shape[2] // size

    def remote(source, target, send, recv, device):
        return pltpu.make_async_remote_copy(
            src_ref=source,
            dst_ref=target,
            send_sem=send,
            recv_sem=recv,
            device_id=device,
            device_id_type=MESH,
        )

    def rows(start, size):
        return pl.ds(pl.multiple_of(start, size), size)

    def drain(block, semaphore):
        pltpu.make_async_copy(block, block, semaphore).wait()

    def guarded(condition, action):
        if condition is None:
            action()
        else:
            pl.when(condition)(action)

    links = [
        (None, {"ctx": other}),
        (None, {"hs": row_peer}),
        (None, {"hs": core_peer}),
        (depth < last, {"hs": me + 4}),
        (depth > 0, {"hs": me - 4}),
    ]
    link_count = 3 + jnp.where(depth < last, 1, 0) + jnp.where(depth > 0, 1, 0)

    def greet(semaphore):
        for condition, device in links:
            guarded(
                condition,
                functools.partial(
                    pl.semaphore_signal, semaphore, inc=1, device_id=device, device_id_type=MESH
                ),
            )

    barrier = pltpu.get_barrier_semaphore()
    greet(barrier)

    weights = (gate_hbm, up_hbm, down_hbm)
    near = rows(ctx * tokens, tokens)
    owned = [
        pltpu.make_async_copy(source, target, local_sem.at[0])
        for source, target in [
            (source.at[0], fast.at[i, rows(ctx * part, part)])
            for i, source in enumerate(weights)
        ]
        + [
            (source.at[0], target.at[near])
            for source, target in ((key_hbm, keys), (value_hbm, values), (query_hbm, queries))
        ]
    ]
    own_rates = pltpu.make_async_copy(rate_hbm, rates.at[ctx], local_sem.at[1])
    side_copy = pltpu.make_async_copy(side_hbm, side, local_sem.at[2])
    own_shard = pltpu.make_async_copy(
        weight_hbm, full.at[rows(me * shard, shard)], local_sem.at[3]
    )
    gain_copy = pltpu.make_async_copy(gain_hbm, gain, local_sem.at[4])

    @pl.when(owner)
    def _():
        for copy in owned:
            copy.start()
        own_rates.start()

    for copy in (side_copy, own_shard, gain_copy):
        copy.start()
    pl.semaphore_wait(barrier, link_count)

    mid = layers // 2
    side_half = (depth // mid) * mid
    order = [mid - side_half + (depth + step) % mid for step in range(mid)]
    order += [side_half + (depth + step) % mid for step in range(1, mid)] + [depth]

    swaps = [(rate_hbm, lambda who: rates.at[who])]
    for i, source in enumerate(weights):
        swaps.append((source.at[0], lambda who, i=i: fast.at[i, rows(who * part, part)]))
    for j in range(pieces):
        for source, target in ((key_hbm.at[0], keys), (value_hbm.at[0], values)):
            swaps.append(
                (
                    source.at[pl.ds(j * piece, piece)],
                    lambda who, target=target, j=j: target.at[
                        rows(who * tokens + j * piece, piece)
                    ],
                )
            )
    for step in range(layers):
        swaps.append(
            (
                query_hbm.at[0, rows(order[step] * step_rows, step_rows)],
                lambda who, step=step: queries.at[
                    rows(who * tokens + order[step] * step_rows, step_rows)
                ],
            )
        )
    arrivals = [0, 1, 1, 1]
    arrivals += [2 + j for j in range(pieces) for _ in range(2)]
    arrivals += [2 + pieces + step for step in range(layers)]
    outgoing = [
        remote(
            source,
            target(ctx),
            ctx_send.at[0 if i == 0 else 1],
            ctx_recv.at[arrivals[i]],
            {"ctx": other},
        )
        for i, (source, target) in enumerate(swaps)
    ]
    def lines(count):
        return full.at[pl.ds(0, count * size // full.shape[1])]

    def held(index):
        return full.at[rows(index * shard, shard)]

    def full_copy(source, index, way, device):
        return remote(source, held(index), full_send.at[way], full_recv.at[index], {"hs": device})

    def arrived(index):
        block = held(index)
        remote(block, block, full_send.at[0], full_recv.at[index], {"hs": core_peer}).wait_recv()

    def start_all(made):
        for condition, copy in made:
            guarded(condition, copy.start)

    first_sends = [
        (None, full_copy(weight_hbm, me, 3, core_peer)),
        (depth < last, full_copy(weight_hbm, me, 0, me + 4)),
        (depth > 0, full_copy(weight_hbm, me, 1, me - 4)),
        (None, full_copy(weight_hbm, me, 2, row_peer)),
    ]
    second_sends = [
        (depth < last, full_copy(held(core_peer), core_peer, 0, me + 4)),
        (depth > 0, full_copy(held(core_peer), core_peer, 1, me - 4)),
        (None, full_copy(held(core_peer), core_peer, 2, row_peer)),
    ]
    relays = []
    for hop in range(1, layers):
        for base in (me, core_peer):
            for upward in (True, False):
                exists = depth >= hop if upward else depth + hop <= last
                onward = depth < last if upward else depth > 0
                index = base - 4 * hop if upward else base + 4 * hop
                next_device = me + 4 if upward else me - 4
                made = [
                    (exists & onward, full_copy(held(index), index, 0 if upward else 1, next_device)),
                    (exists, full_copy(held(index), index, 2, row_peer)),
                    (exists, full_copy(held(index), index, 3, core_peer)),
                ]
                relays.append((hop, exists, index, made))
    crossed = []
    for step in range(layers):
        for base in (row_peer, depth * 4 + (1 - row) * 2 + (1 - core)):
            index = (base + 4 * step) % count
            crossed.append((index, full_copy(held(index), index, 3, core_peer)))

    own_copy = remote(
        weight_hbm, held(me), full_send.at[3], full_recv.at[me], {"hs": core_peer}
    )

    @pl.when(owner)
    def _():
        own_copy.start()

    @pl.when(helper)
    def _():
        for copy in outgoing:
            copy.start()
        start_all(first_sends)

    for i in range(max(2, layers - 2)):
        greet(ready.at[i])
        pl.semaphore_wait(ready.at[i], link_count)

    @pl.when(helper)
    def _():
        arrived(core_peer)
        start_all(second_sends)

    side_copy.wait()
    spread = side[...].astype(jnp.float32)
    for seq in range(seq_count):
        moved[seq] = spread[:, seq, :].astype(jnp.bfloat16)
    gate_copies = [
        remote(
            moved.at[order[step]],
            gates.at[depth],
            gate_send,
            gate_recv.at[depth],
            {"hs": order[step] * 4 + inner},
        )
        for step in range(last)
    ]

    def start_gates(outermost):
        for step, copy in enumerate(gate_copies):
            target = order[step]
            outer = (target == 0) | (target == last)
            pl.when(outer if outermost else jnp.logical_not(outer))(copy.start)

    @pl.when(helper)
    def _():
        for position, (hop, exists, index, made) in enumerate(relays):
            pl.when(exists)(functools.partial(arrived, index))
            start_all(made)
            if position + 1 == 4 * max(1, layers - 2):
                start_gates(False)
        for turn, (index, copy) in enumerate(crossed):
            if turn == layers:
                start_gates(True)
            arrived(index)
            copy.start()

    def learn(start, rate, first):
        key_part = keys[rows(start, piece), :]
        rate_column = jnp.broadcast_to(rate, (128, piece)).T[:, :1]
        scaled_part = (rate_column * values[rows(start, piece), :].astype(jnp.float32)).astype(
            jnp.bfloat16
        )
        pre_gate = inner_cols(key_part, fast[0])
        pre_up = inner_cols(key_part, fast[1])
        sig_gate = jax.nn.sigmoid(pre_gate)
        act_gate = pre_gate * sig_gate
        hidden = (act_gate * pre_up).astype(jnp.bfloat16)
        back_hidden = jnp.dot(scaled_part, fast[2], preferred_element_type=jnp.float32)
        back_gate = (
            back_hidden * pre_up * sig_gate * (1.0 + pre_gate * (1.0 - sig_gate))
        ).astype(jnp.bfloat16)
        back_up = (back_hidden * act_gate).astype(jnp.bfloat16)
        terms = (
            inner_rows(back_gate, key_part),
            inner_rows(back_up, key_part),
            inner_rows(scaled_part, hidden),
        )
        for i, term in enumerate(terms):
            grads[i] = term if first else grads[i] + term

    head_copies = {}
    for half in (other, ctx):
        for step in range(layers):
            start = half * tokens + order[step] * step_rows
            for i in range(3 if half is ctx else 4):
                place = (inner + 1 + i) % 4
                head_copies[half is ctx, step, i] = remote(
                    heads.at[rows(start + place * block_rows, block_rows)],
                    mixed.at[order[step], row * 2 + ctx],
                    head_send,
                    head_recv.at[order[step]],
                    {"ctx": half, "hs": depth * 4 + place},
                )

    def answer(half, step):
        target = order[step]
        start = half * tokens + target * step_rows
        query_part = queries[rows(start, step_rows), :]
        query_gate = inner_cols(query_part, fresh[0])
        query_up = inner_cols(query_part, fresh[1])
        query_hidden = (query_gate * jax.nn.sigmoid(query_gate) * query_up).astype(jnp.bfloat16)
        heads[rows(start, step_rows), :] = inner_cols(query_hidden, fresh[2]).astype(jnp.bfloat16)
        for i in range(4):
            if half is ctx and i == 3:
                mixed[target, row * 2 + ctx] = heads[
                    rows(start + inner * block_rows, block_rows), :
                ]
            else:
                head_copies[half is ctx, step, i].start()

    @pl.when(owner)
    def _():
        drain(lines(3 * part + 3 * tokens), local_sem.at[0])
        own_rates.wait()
        drain(lines(3 * part), ctx_recv.at[1])
        for j in range(pieces):
            learn(ctx * tokens + j * piece, rates[ctx, :, j * piece : (j + 1) * piece], j == 0)
        start_gates(False)
        drain(rates.at[other], ctx_recv.at[0])
        for j in range(pieces):
            drain(lines(2 * piece), ctx_recv.at[2 + j])
            if j == pieces - 1:
                start_gates(True)
            learn(
                other * tokens + j * piece, rates[other, :, j * piece : (j + 1) * piece], False
            )
        for i in range(3):
            fresh[i] = rescale_rows(fast[i], grads[i])
        for step in range(layers):
            drain(lines(step_rows), ctx_recv.at[2 + pieces + step])
            answer(other, step)
            answer(ctx, step)
        for step in range(1, count):
            arrived((me + step) % count)

    own_shard.wait()
    gain_copy.wait()
    for step in range(layers):
        target = order[step]

        @pl.when(owner)
        def _():
            drain(mixed.at[target, pl.ds(0, 3)], head_recv.at[target])

        @pl.when(helper)
        def _():
            drain(mixed.at[target], head_recv.at[target])

        if step < last:
            drain(gates.at[target], gate_recv.at[target])
            opened = gates[target]
        else:
            opened = moved[depth]
        opened = opened.astype(jnp.float32)
        opened = opened * jax.nn.sigmoid(opened)
        for head in range(head_count):
            columns = slice(head * size, (head + 1) * size)
            value = mixed[target, head].astype(jnp.float32)
            square = jnp.mean(value * value, -1, keepdims=True)
            value = value * lax.rsqrt(square + epsilon) * gain[:, columns]
            normed[step, :, columns] = (value * opened[:, columns]).astype(jnp.bfloat16)
        result = jnp.dot(normed[step], full[...], preferred_element_type=jnp.float32)
        outs[step] = result.astype(jnp.bfloat16)
        if step < last:
            copy = remote(
                outs.at[step],
                out_ref.at[depth],
                out_send,
                out_recv,
                {"hs": target * 4 + inner},
            )
        else:
            copy = pltpu.make_async_copy(outs.at[step], out_ref.at[depth], local_sem.at[2])
        copy.start()

    @pl.when(owner)
    def _():
        drain(held(0), full_send.at[3])
        drain(heads.at[pl.ds(0, 7 * layers * block_rows)], head_send)

    def sent(amount, way):
        if amount:
            drain(full.at[pl.ds(0, amount * shard)], full_send.at[way])

    @pl.when(helper)
    def _():
        drain(rates.at[ctx], ctx_send.at[0])
        drain(lines(3 * part + 3 * tokens), ctx_send.at[1])
        for layer in range(layers):

            @pl.when(depth == layer)
            def _():
                sent(2 + 2 * layer if layer < last else 0, 0)
                sent(2 + 2 * (last - layer) if layer > 0 else 0, 1)

        sent(2 * layers, 2)
        sent(4 * layers - 1, 3)

    drain(moved.at[pl.ds(0, last)], gate_send)
    drain(outs.at[pl.ds(0, last)], out_send)
    drain(outs.at[pl.ds(0, last)], out_recv)
    drain(outs.at[0], local_sem.at[2])


def swapped_body(
    key_rows,
    value_rows,
    query_rows,
    step_rates,
    fast_gate,
    fast_up,
    fast_down,
    out_gain,
    gate_input,
    out_weight,
):
    layers = lax.axis_size("hs") // 4
    count = 4 * layers
    pieces = 2
    tokens, size = key_rows.shape[1:]
    hidden_size = 2 * fast_gate.shape[1]
    block_rows, seq_count, width = gate_input.shape
    columns = out_weight.shape[1]
    anywhere = pl.BlockSpec(memory_space=pl.ANY)
    half = jnp.bfloat16
    dma = pltpu.SemaphoreType.DMA
    laid = pl.pallas_call(
        functools.partial(layer_kernel, layers, pieces),
        out_shape=jax.ShapeDtypeStruct((seq_count, block_rows, columns), half),
        in_specs=[anywhere] * 10,
        out_specs=anywhere,
        scratch_shapes=[
            pltpu.VMEM((3, hidden_size, size), half),
            pltpu.VMEM((3, hidden_size, size), half),
            pltpu.VMEM((2 * tokens, size), half),
            pltpu.VMEM((2 * tokens, size), half),
            pltpu.VMEM((2, 1, tokens), jnp.float32),
            pltpu.VMEM((2 * tokens, size), half),
            pltpu.VMEM((1, width), jnp.float32),
            pltpu.VMEM((block_rows, seq_count, width), half),
            pltpu.VMEM((seq_count, block_rows, width), half),
            pltpu.VMEM((layers, block_rows, width), half),
            pltpu.VMEM((width, columns), half),
            pltpu.VMEM((3, hidden_size, size), jnp.float32),
            pltpu.VMEM((2 * tokens, size), half),
            pltpu.VMEM((layers, 4, block_rows, size), half),
            pltpu.VMEM((layers, block_rows, width), half),
            pltpu.VMEM((layers, block_rows, columns), half),
            dma((5,)),
            dma((2,)),
            dma((2 + pieces + layers,)),
            dma((4,)),
            dma((count,)),
            dma(()),
            dma((layers,)),
            dma(()),
            dma((layers,)),
            dma(()),
            dma(()),
            pltpu.SemaphoreType.REGULAR((max(2, layers - 2),)),
        ],
        compiler_params=pltpu.CompilerParams(
            collective_id=0, has_side_effects=True, vmem_limit_bytes=60 * 1024 * 1024
        ),
    )(
        fast_gate,
        fast_up,
        fast_down,
        key_rows,
        value_rows,
        query_rows,
        gate_input,
        out_weight,
        step_rates,
        out_gain[None],
    )
    return laid.transpose(1, 0, 2)


def solution(mesh):
    def step(*arrays):
        paired = mesh.shape["ctx"] == 2 and mesh.shape["hs"] % 8 == 0
        paired = paired and arrays[0].shape[0] == 1
        paired = paired and arrays[8].shape[1] == mesh.shape["hs"] // 4
        paired = paired and arrays[8].shape[2] == 4 * arrays[0].shape[2]
        return (swapped_body if paired else body)(*arrays)

    return jax.shard_map(
        step,
        mesh=mesh,
        in_specs=(
            P("hs", "ctx", None),
            P("hs", "ctx", None),
            P("hs", "ctx", None),
            P("hs", "ctx"),
            P("hs", "ctx", None),
            P("hs", "ctx", None),
            P("hs", "ctx", None),
            P(),
            P(("ctx", "hs"), None, None),
            P("hs", None),
        ),
        out_specs=P(("ctx", "hs"), None, None),
        check_vma=False,
    )
```

```python
import functools
import math

import jax
import jax.numpy as jnp
from jax import lax
from jax.experimental import pallas as pl
from jax.experimental.pallas import tpu as pltpu
from jax.sharding import PartitionSpec as P

epsilon = 1e-06


def rescale_rows(weight, update):
    base = weight.astype(jnp.float32)
    moved = base + update
    factor = jnp.sqrt(jnp.mean(base * base, -1, keepdims=True) + epsilon) / jnp.sqrt(
        jnp.mean(moved * moved, -1, keepdims=True) + epsilon
    )
    return (moved * factor).astype(jnp.bfloat16)


def inner_rows(left, right):
    return lax.dot_general(
        left, right, (((0,), (0,)), ((), ())), preferred_element_type=jnp.float32
    )


def body(
    key_rows,
    value_rows,
    query_rows,
    step_rates,
    fast_gate,
    fast_up,
    fast_down,
    out_gain,
    gate_input,
    out_weight,
):
    key_row = key_rows[0]
    value_row = value_rows[0]
    query_row = query_rows[0]
    rate_row = step_rates[0]
    whole_gate, whole_up, whole_down = (
        lax.all_gather(fast_gate, "ctx", axis=1, tiled=True),
        lax.all_gather(fast_up, "ctx", axis=1, tiled=True),
        lax.all_gather(fast_down, "ctx", axis=1, tiled=True),
    )
    gate_fast = whole_gate[0]
    up_fast = whole_up[0]
    down_fast = whole_down[0]
    pre_gate = jnp.dot(key_row, gate_fast.T, preferred_element_type=jnp.float32)
    pre_up = jnp.dot(key_row, up_fast.T, preferred_element_type=jnp.float32)
    sig_gate = jax.nn.sigmoid(pre_gate)
    act_gate = pre_gate * sig_gate
    hidden = (act_gate * pre_up).astype(jnp.bfloat16)
    scaled = (rate_row[:, None] * value_row.astype(jnp.float32)).astype(jnp.bfloat16)
    grad_down = inner_rows(scaled, hidden)
    back_hidden = jnp.dot(scaled, down_fast, preferred_element_type=jnp.float32)
    back_gate = (back_hidden * pre_up * sig_gate * (1.0 + pre_gate * (1.0 - sig_gate))).astype(
        jnp.bfloat16
    )
    back_up = (back_hidden * act_gate).astype(jnp.bfloat16)
    grad_gate = inner_rows(back_gate, key_row)
    grad_up = inner_rows(back_up, key_row)
    grad_gate, grad_up, grad_down = (
        lax.psum_scatter(grad_gate, "ctx", scatter_dimension=0, tiled=True),
        lax.psum_scatter(grad_up, "ctx", scatter_dimension=0, tiled=True),
        lax.psum_scatter(grad_down, "ctx", scatter_dimension=0, tiled=True),
    )
    part_gate = rescale_rows(fast_gate[0], grad_gate)
    part_up = rescale_rows(fast_up[0], grad_up)
    part_down = rescale_rows(fast_down[0], grad_down)
    new_gate, new_up, new_down = (
        lax.all_gather(part_gate, "ctx", axis=0, tiled=True),
        lax.all_gather(part_up, "ctx", axis=0, tiled=True),
        lax.all_gather(part_down, "ctx", axis=0, tiled=True),
    )
    query_gate = jnp.dot(query_row, new_gate.T, preferred_element_type=jnp.float32)
    query_up = jnp.dot(query_row, new_up.T, preferred_element_type=jnp.float32)
    query_hidden = (jax.nn.silu(query_gate) * query_up).astype(jnp.bfloat16)
    head_out = jnp.dot(query_hidden, new_down.T, preferred_element_type=jnp.float32).astype(
        jnp.bfloat16
    )
    width_hs = lax.axis_size("hs")
    head_size = head_out.shape[1]
    token_count = head_out.shape[0] // width_hs
    blocks = head_out.reshape(width_hs, token_count, head_size)
    moved = lax.all_to_all(blocks, "hs", split_axis=0, concat_axis=2, tiled=True)
    seq_count = gate_input.shape[1]
    model_width = gate_input.shape[2]
    head_count = model_width // head_size
    mixed = moved.reshape(token_count, seq_count, head_count, head_size).astype(jnp.float32)
    square = jnp.mean(mixed * mixed, -1, keepdims=True)
    scaled_heads = mixed * lax.rsqrt(square + epsilon) * out_gain.reshape(head_count, head_size)
    normed = (
        scaled_heads.reshape(token_count, seq_count, model_width)
        * jax.nn.silu(gate_input.astype(jnp.float32))
    ).astype(jnp.bfloat16)
    flat_rows = normed.reshape(token_count * seq_count, model_width)
    out_cols = out_weight.shape[1]
    full_weight = lax.all_gather(out_weight, "hs", axis=0, tiled=True)
    result = jnp.dot(flat_rows, full_weight, preferred_element_type=jnp.float32)
    return result.astype(jnp.bfloat16).reshape(token_count, seq_count, out_cols)


MESH = pl.DeviceIdType.MESH


def inner_cols(left, right):
    return lax.dot_general(
        left, right, (((1,), (1,)), ((), ())), preferred_element_type=jnp.float32
    )


def layer_kernel(
    layers,
    pieces,
    gate_hbm,
    up_hbm,
    down_hbm,
    key_hbm,
    value_hbm,
    query_hbm,
    side_hbm,
    weight_hbm,
    rate_hbm,
    gain_hbm,
    out_ref,
    fast,
    fresh,
    keys,
    values,
    rates,
    queries,
    gain,
    side,
    moved,
    gates,
    full,
    grads,
    heads,
    mixed,
    normed,
    outs,
    local_sem,
    ctx_send,
    ctx_recv,
    full_send,
    full_recv,
    gate_send,
    gate_recv,
    head_send,
    head_recv,
    out_send,
    out_recv,
    ready,
):
    ctx = lax.axis_index("ctx")
    me = lax.axis_index("hs")
    other = 1 - ctx
    count = 4 * layers
    last = layers - 1
    depth, inner = me // 4, me % 4
    row, core = inner // 2, inner % 2
    row_peer = depth * 4 + (1 - row) * 2 + core
    core_peer = depth * 4 + row * 2 + (1 - core)
    owner = core == ctx
    helper = core != ctx
    part = gate_hbm.shape[1]
    tokens = key_hbm.shape[1]
    piece = tokens // pieces
    shard = weight_hbm.shape[0]
    block_rows = tokens // count
    step_rows = 4 * block_rows
    seq_count = side.shape[1]
    size = key_hbm.shape[2]
    head_count = side.shape[2] // size

    def remote(source, target, send, recv, device):
        return pltpu.make_async_remote_copy(
            src_ref=source,
            dst_ref=target,
            send_sem=send,
            recv_sem=recv,
            device_id=device,
            device_id_type=MESH,
        )

    def rows(start, size):
        return pl.ds(pl.multiple_of(start, math.gcd(size, 128)), size)

    def drain(block, semaphore):
        pltpu.make_async_copy(block, block, semaphore).wait()

    def guarded(condition, action):
        if condition is None:
            action()
        else:
            pl.when(condition)(action)

    links = [
        (None, {"ctx": other}),
        (None, {"hs": row_peer}),
        (None, {"hs": core_peer}),
        (depth < last, {"hs": me + 4}),
        (depth > 0, {"hs": me - 4}),
    ]
    link_count = 3 + jnp.where(depth < last, 1, 0) + jnp.where(depth > 0, 1, 0)

    def greet(semaphore):
        for condition, device in links:
            guarded(
                condition,
                functools.partial(
                    pl.semaphore_signal, semaphore, inc=1, device_id=device, device_id_type=MESH
                ),
            )

    barrier = pltpu.get_barrier_semaphore()
    greet(barrier)

    weights = (gate_hbm, up_hbm, down_hbm)
    near = rows(ctx * tokens, tokens)
    owned = [
        pltpu.make_async_copy(source, target, local_sem.at[0])
        for source, target in [
            (source.at[0], fast.at[i, rows(ctx * part, part)])
            for i, source in enumerate(weights)
        ]
        + [
            (source.at[0], target.at[near])
            for source, target in ((key_hbm, keys), (value_hbm, values), (query_hbm, queries))
        ]
    ]
    own_rates = pltpu.make_async_copy(rate_hbm, rates.at[ctx], local_sem.at[1])
    side_copy = pltpu.make_async_copy(side_hbm, side, local_sem.at[2])
    own_shard = pltpu.make_async_copy(
        weight_hbm, full.at[rows(me * shard, shard)], local_sem.at[3]
    )
    gain_copy = pltpu.make_async_copy(gain_hbm, gain, local_sem.at[4])

    @pl.when(owner)
    def _():
        for copy in owned:
            copy.start()
        own_rates.start()

    for copy in (side_copy, own_shard, gain_copy):
        copy.start()
    pl.semaphore_wait(barrier, link_count)

    mid = layers // 2
    side_half = (depth // mid) * mid
    order = [mid - side_half + (depth + step) % mid for step in range(mid)]
    order += [side_half + (depth + step) % mid for step in range(1, mid)] + [depth]

    swaps = [(rate_hbm, lambda who: rates.at[who])]
    for i, source in enumerate(weights):
        swaps.append((source.at[0], lambda who, i=i: fast.at[i, rows(who * part, part)]))
    for j in range(pieces):
        for source, target in ((key_hbm.at[0], keys), (value_hbm.at[0], values)):
            swaps.append(
                (
                    source.at[pl.ds(j * piece, piece)],
                    lambda who, target=target, j=j: target.at[
                        rows(who * tokens + j * piece, piece)
                    ],
                )
            )
    for step in range(layers):
        swaps.append(
            (
                query_hbm.at[0, rows(order[step] * step_rows, step_rows)],
                lambda who, step=step: queries.at[
                    rows(who * tokens + order[step] * step_rows, step_rows)
                ],
            )
        )
    arrivals = [0, 1, 1, 1]
    arrivals += list(range(2, 2 + 2 * pieces + layers))
    outgoing = [
        remote(
            source,
            target(ctx),
            ctx_send.at[0 if i == 0 else 1],
            ctx_recv.at[arrivals[i]],
            {"ctx": other},
        )
        for i, (source, target) in enumerate(swaps)
    ]
    def lines(count):
        return full.at[pl.ds(0, count * size // full.shape[1])]

    def held(index):
        return full.at[rows(index * shard, shard)]

    def full_copy(source, index, way, device):
        return remote(source, held(index), full_send.at[way], full_recv.at[index], {"hs": device})

    def arrived(index):
        block = held(index)
        remote(block, block, full_send.at[0], full_recv.at[index], {"hs": core_peer}).wait_recv()

    def start_all(made):
        for condition, copy in made:
            guarded(condition, copy.start)

    first_sends = [
        (None, full_copy(weight_hbm, me, 3, core_peer)),
        (depth < last, full_copy(weight_hbm, me, 0, me + 4)),
        (depth > 0, full_copy(weight_hbm, me, 1, me - 4)),
        (None, full_copy(weight_hbm, me, 2, row_peer)),
    ]
    second_sends = [
        (depth < last, full_copy(held(core_peer), core_peer, 0, me + 4)),
        (depth > 0, full_copy(held(core_peer), core_peer, 1, me - 4)),
        (None, full_copy(held(core_peer), core_peer, 2, row_peer)),
    ]
    relays = []
    for hop in range(1, layers):
        for base in (me, core_peer):
            for upward in (True, False):
                exists = depth >= hop if upward else depth + hop <= last
                onward = depth < last if upward else depth > 0
                index = base - 4 * hop if upward else base + 4 * hop
                next_device = me + 4 if upward else me - 4
                made = [
                    (exists & onward, full_copy(held(index), index, 0 if upward else 1, next_device)),
                    (exists, full_copy(held(index), index, 2, row_peer)),
                    (exists, full_copy(held(index), index, 3, core_peer)),
                ]
                relays.append((hop, exists, index, made))
    crossed = []
    for step in range(layers):
        for base in (row_peer, depth * 4 + (1 - row) * 2 + (1 - core)):
            index = (base + 4 * step) % count
            crossed.append((index, full_copy(held(index), index, 3, core_peer)))

    own_copy = remote(
        weight_hbm, held(me), full_send.at[3], full_recv.at[me], {"hs": core_peer}
    )

    @pl.when(owner)
    def _():
        own_copy.start()

    @pl.when(helper)
    def _():
        for copy in outgoing:
            copy.start()
        start_all(first_sends)

    for i in range(max(2, layers - 2)):
        greet(ready.at[i])
        pl.semaphore_wait(ready.at[i], link_count)

    @pl.when(helper)
    def _():
        arrived(core_peer)
        start_all(second_sends)

    side_copy.wait()
    spread = side[...].astype(jnp.float32)
    for seq in range(seq_count):
        moved[seq] = spread[:, seq, :].astype(jnp.bfloat16)
    gate_copies = [
        remote(
            moved.at[order[step]],
            gates.at[depth],
            gate_send,
            gate_recv.at[depth],
            {"hs": order[step] * 4 + inner},
        )
        for step in range(last)
    ]

    def start_gates(outermost):
        for step, copy in enumerate(gate_copies):
            target = order[step]
            outer = (target == 0) | (target == last)
            pl.when(outer if outermost else jnp.logical_not(outer))(copy.start)

    @pl.when(helper)
    def _():
        for position, (hop, exists, index, made) in enumerate(relays):
            pl.when(exists)(functools.partial(arrived, index))
            start_all(made)
            if position + 1 == 4 * max(1, layers - 2):
                start_gates(False)
        for turn, (index, copy) in enumerate(crossed):
            if turn == layers:
                start_gates(True)
            arrived(index)
            copy.start()

    def forward(start):
        key_part = keys[rows(start, piece), :]
        pre_gate = inner_cols(key_part, fast[0])
        pre_up = inner_cols(key_part, fast[1])
        sig_gate = jax.nn.sigmoid(pre_gate)
        act_gate = pre_gate * sig_gate
        hidden = (act_gate * pre_up).astype(jnp.bfloat16)
        slope = pre_up * sig_gate * (1.0 + pre_gate * (1.0 - sig_gate))
        return key_part, act_gate, hidden, slope

    def backward(start, rate, made):
        key_part, act_gate, hidden, slope = made
        rate_column = jnp.broadcast_to(rate, (128, piece)).T[:, :1]
        scaled_part = (rate_column * values[rows(start, piece), :].astype(jnp.float32)).astype(
            jnp.bfloat16
        )
        back_hidden = jnp.dot(scaled_part, fast[2], preferred_element_type=jnp.float32)
        back_gate = (back_hidden * slope).astype(jnp.bfloat16)
        back_up = (back_hidden * act_gate).astype(jnp.bfloat16)
        return (
            lambda: inner_rows(back_gate, key_part),
            lambda: inner_rows(back_up, key_part),
            lambda: inner_rows(scaled_part, hidden),
        )

    head_copies = {}
    for half in (other, ctx):
        for step in range(layers):
            start = half * tokens + order[step] * step_rows
            for i in range(3 if half is ctx else 4):
                place = (inner + 1 + i) % 4
                head_copies[half is ctx, step, i] = remote(
                    heads.at[rows(start + place * block_rows, block_rows)],
                    mixed.at[order[step], row * 2 + ctx],
                    head_send,
                    head_recv.at[order[step]],
                    {"ctx": half, "hs": depth * 4 + place},
                )

    def answer(half, steps, first, amount):
        span = rows(half * tokens + first * step_rows, step_rows * amount)
        query_part = queries[span, :]
        query_gate = inner_cols(query_part, fresh[0])
        query_up = inner_cols(query_part, fresh[1])
        query_hidden = (query_gate * jax.nn.sigmoid(query_gate) * query_up).astype(jnp.bfloat16)
        heads[span, :] = inner_cols(query_hidden, fresh[2]).astype(jnp.bfloat16)
        for step in steps:
            target = order[step]
            for i in range(4):
                if half is ctx and i == 3:
                    start = half * tokens + target * step_rows
                    mixed[target, row * 2 + ctx] = heads[
                        rows(start + inner * block_rows, block_rows), :
                    ]
                else:
                    head_copies[half is ctx, step, i].start()

    @pl.when(owner)
    def _():
        drain(lines(3 * part + 3 * tokens), local_sem.at[0])
        own_rates.wait()
        drain(lines(3 * part), ctx_recv.at[1])
        for j in range(pieces):
            start = ctx * tokens + j * piece
            rate = rates[ctx, :, j * piece : (j + 1) * piece]
            for i, term in enumerate(backward(start, rate, forward(start))):
                grads[i] = term() if j == 0 else grads[i] + term()
        start_gates(False)
        drain(rates.at[other], ctx_recv.at[0])
        for j in range(pieces):
            start = other * tokens + j * piece
            drain(lines(piece), ctx_recv.at[2 + 2 * j])
            drain(lines(piece), ctx_recv.at[3 + 2 * j])
            made = forward(start)
            if j == pieces - 1:
                start_gates(True)
            rate = rates[other, :, j * piece : (j + 1) * piece]
            for i, term in enumerate(backward(start, rate, made)):
                grads[i] = grads[i] + term()
        for i in range(3):
            fresh[i] = rescale_rows(fast[i], grads[i])
        for step in range(layers):
            drain(lines(step_rows), ctx_recv.at[2 + 2 * pieces + step])
            answer(other, [step], order[step], 1)
            if step == 0:
                answer(ctx, range(mid), mid - side_half, mid)
            if step == min(1, last - 1):
                answer(ctx, range(mid, layers), side_half, mid)
        for step in range(1, count):
            arrived((me + step) % count)

    own_shard.wait()
    gain_copy.wait()
    for step in range(layers):
        target = order[step]

        @pl.when(owner)
        def _():
            drain(mixed.at[target, pl.ds(0, 3)], head_recv.at[target])

        @pl.when(helper)
        def _():
            drain(mixed.at[target], head_recv.at[target])

        if step < last:
            drain(gates.at[target], gate_recv.at[target])
            opened = gates[target]
        else:
            opened = moved[depth]
        opened = opened.astype(jnp.float32)
        opened = opened * jax.nn.sigmoid(opened)
        for head in range(head_count):
            columns = slice(head * size, (head + 1) * size)
            value = mixed[target, head].astype(jnp.float32)
            square = jnp.mean(value * value, -1, keepdims=True)
            value = value * lax.rsqrt(square + epsilon) * gain[:, columns]
            normed[step, :, columns] = (value * opened[:, columns]).astype(jnp.bfloat16)
        result = jnp.dot(normed[step], full[...], preferred_element_type=jnp.float32)
        outs[step] = result.astype(jnp.bfloat16)
        if step < last:
            copy = remote(
                outs.at[step],
                out_ref.at[depth],
                out_send,
                out_recv,
                {"hs": target * 4 + inner},
            )
        else:
            copy = pltpu.make_async_copy(outs.at[step], out_ref.at[depth], local_sem.at[2])
        copy.start()

    @pl.when(owner)
    def _():
        drain(held(0), full_send.at[3])
        drain(heads.at[pl.ds(0, 7 * layers * block_rows)], head_send)

    def sent(amount, way):
        if amount:
            drain(full.at[pl.ds(0, amount * shard)], full_send.at[way])

    @pl.when(helper)
    def _():
        drain(rates.at[ctx], ctx_send.at[0])
        drain(lines(3 * part + 3 * tokens), ctx_send.at[1])
        for layer in range(layers):

            @pl.when(depth == layer)
            def _():
                sent(2 + 2 * layer if layer < last else 0, 0)
                sent(2 + 2 * (last - layer) if layer > 0 else 0, 1)

        sent(2 * layers, 2)
        sent(4 * layers - 1, 3)

    drain(moved.at[pl.ds(0, last)], gate_send)
    drain(outs.at[pl.ds(0, last)], out_send)
    drain(outs.at[pl.ds(0, last)], out_recv)
    drain(outs.at[0], local_sem.at[2])


def swapped_body(
    key_rows,
    value_rows,
    query_rows,
    step_rates,
    fast_gate,
    fast_up,
    fast_down,
    out_gain,
    gate_input,
    out_weight,
):
    layers = lax.axis_size("hs") // 4
    count = 4 * layers
    pieces = 2
    tokens, size = key_rows.shape[1:]
    hidden_size = 2 * fast_gate.shape[1]
    block_rows, seq_count, width = gate_input.shape
    columns = out_weight.shape[1]
    anywhere = pl.BlockSpec(memory_space=pl.ANY)
    half = jnp.bfloat16
    dma = pltpu.SemaphoreType.DMA
    laid = pl.pallas_call(
        functools.partial(layer_kernel, layers, pieces),
        out_shape=jax.ShapeDtypeStruct((seq_count, block_rows, columns), half),
        in_specs=[anywhere] * 10,
        out_specs=anywhere,
        scratch_shapes=[
            pltpu.VMEM((3, hidden_size, size), half),
            pltpu.VMEM((3, hidden_size, size), half),
            pltpu.VMEM((2 * tokens, size), half),
            pltpu.VMEM((2 * tokens, size), half),
            pltpu.VMEM((2, 1, tokens), jnp.float32),
            pltpu.VMEM((2 * tokens, size), half),
            pltpu.VMEM((1, width), jnp.float32),
            pltpu.VMEM((block_rows, seq_count, width), half),
            pltpu.VMEM((seq_count, block_rows, width), half),
            pltpu.VMEM((layers, block_rows, width), half),
            pltpu.VMEM((width, columns), half),
            pltpu.VMEM((3, hidden_size, size), jnp.float32),
            pltpu.VMEM((2 * tokens, size), half),
            pltpu.VMEM((layers, 4, block_rows, size), half),
            pltpu.VMEM((layers, block_rows, width), half),
            pltpu.VMEM((layers, block_rows, columns), half),
            dma((5,)),
            dma((2,)),
            dma((2 + 2 * pieces + layers,)),
            dma((4,)),
            dma((count,)),
            dma(()),
            dma((layers,)),
            dma(()),
            dma((layers,)),
            dma(()),
            dma(()),
            pltpu.SemaphoreType.REGULAR((max(2, layers - 2),)),
        ],
        compiler_params=pltpu.CompilerParams(
            collective_id=0, has_side_effects=True, vmem_limit_bytes=60 * 1024 * 1024
        ),
    )(
        fast_gate,
        fast_up,
        fast_down,
        key_rows,
        value_rows,
        query_rows,
        gate_input,
        out_weight,
        step_rates,
        out_gain[None],
    )
    return laid.transpose(1, 0, 2)


def solution(mesh):
    def step(*arrays):
        paired = mesh.shape["ctx"] == 2 and mesh.shape["hs"] % 8 == 0
        paired = paired and arrays[0].shape[0] == 1
        paired = paired and arrays[8].shape[1] == mesh.shape["hs"] // 4
        paired = paired and arrays[8].shape[2] == 4 * arrays[0].shape[2]
        return (swapped_body if paired else body)(*arrays)

    return jax.shard_map(
        step,
        mesh=mesh,
        in_specs=(
            P("hs", "ctx", None),
            P("hs", "ctx", None),
            P("hs", "ctx", None),
            P("hs", "ctx"),
            P("hs", "ctx", None),
            P("hs", "ctx", None),
            P("hs", "ctx", None),
            P(),
            P(("ctx", "hs"), None, None),
            P("hs", None),
        ),
        out_specs=P(("ctx", "hs"), None, None),
        check_vma=False,
    )
```
